32 devices in a mesh: rep: 8 (over y, x, core), shard: 4 (over z).
Axes of the slice: x: 2, y: 2, z: 4, core: 2. Of those that a mesh axis runs over, the one named last changes fastest.
Arguments:
- queries: bfloat16 [4096, 4096], P(('rep', 'shard')), may hold values from -120 to 120
- keys: bfloat16 [4096, 512], P(('rep', 'shard')), may hold values from -5.5 to 5.5
- grad_out: bfloat16 [4096, 4096], P(('rep', 'shard')), may hold values from -3 to 3
- inputs: bfloat16 [4096, 8192], P(('rep', 'shard')), may hold values from -6 to 6
- old_owner: int32 [64], replicated, may hold values from 0 to 2, as said below
- new_owner: int32 [64], replicated, may hold values from 0 to 3, as said below
- param_old: float32 [128, 88, 512], P('rep', 'shard'), may hold values from -0.75 to 0.75
- first_old: float32 [128, 88, 512], P('rep', 'shard'), may hold values from -6 to 6
- second_old: float32 [128, 88, 512], P('rep', 'shard'), may hold values from 0.5 to 20
Outputs:
- param_new: float32 [128, 64, 512], P('rep', 'shard')
- first_new: float32 [128, 64, 512], P('rep', 'shard')
- second_new: float32 [128, 64, 512], P('rep', 'shard')
- weights: bfloat16 [128, 64, 512], P('rep')
The draws below stay inside these ranges and needn't reach their ends.
Inputs may be any that keep to these rules, and one draw needn't show every extreme that they name: `old_owner`: each old owner holds at most 22 blocks, and some hold exactly 22. `new_owner`: each new owner holds exactly 16 blocks.
All inputs are finite; a program needn't handle non-finite values.
Results may differ from the reference program's by a relative error of at most 0.0034.
Values may be sent and summed in bfloat16 or wider, within the bound.
A program may use at most 128 MiB of HBM per device.

```python
import math
import jax
import jax.numpy as jnp
from jax import lax

D = 8192
HEADS = 32
KV = 4
HD = 128
GRP = 8
LENGTH = 512
TOKENS = 4096
BLOCKS = 64
BROWS = 128
OLD = 3
OLD_CAP = 22
NEW_CAP = 16
STEP = 1000
N_SHARD = 4


def paired_draw(key):
    seq_count = TOKENS // LENGTH
    key_values = jnp.clip(jax.random.normal(jax.random.fold_in(key, 11), (seq_count, LENGTH, KV, HD), jnp.float32), -4.5, 4.5)
    query_values = jnp.clip(jax.random.normal(jax.random.fold_in(key, 12), (seq_count, LENGTH, KV, GRP, HD), jnp.float32), -4.5, 4.5)
    return (query_values.reshape(TOKENS, HEADS * HD), key_values.reshape(TOKENS, KV * HD))


def draw_queries(key, part):
    return paired_draw(key)[0].astype(jnp.bfloat16)


def draw_keys(key, part):
    return paired_draw(key)[1].astype(jnp.bfloat16)


def draw_old_owner(key, part):
    shuffled = jax.random.permutation(jax.random.fold_in(key, 21), BLOCKS)
    inverse = jnp.argsort(shuffled)
    return (inverse % OLD).astype(jnp.int32)


def draw_new_owner(key, part):
    shuffled = jax.random.permutation(jax.random.fold_in(key, 22), BLOCKS)
    inverse = jnp.argsort(shuffled)
    return (inverse // NEW_CAP).astype(jnp.int32)


def shard_levels(own_key, shape, split, low, high):
    def one(axis_at, shards_of):
        heights = jax.random.uniform(jax.random.fold_in(jax.random.fold_in(own_key, 6), axis_at), (shards_of,), jnp.float32, low / len(split), high / len(split))
        return jnp.repeat(jnp.exp(heights), shape[axis_at] // shards_of).reshape((-1,) + (1,) * (len(shape) - axis_at - 1))

    level = one(*split[0])
    for cut in split[1:]:
        level = level * one(*cut)
    return level


def centred(own_key, dims, scale, most, shards=(), kind=jnp.bfloat16):
    entries = jax.random.normal(own_key, dims, jnp.float32) * scale
    if len(shards) > 0:
        entries = shard_levels(own_key, dims, shards, -0.22, 0.18) * entries
    return jnp.clip(entries, min=-most, max=most).astype(kind)


def setup_inputs(seed: int = 0) -> dict:
    splits = jax.random.split(jax.random.key(seed), 10)
    return {
        "queries": draw_queries(jax.random.fold_in(splits[9], 71), 0),
        "keys": draw_keys(jax.random.fold_in(splits[9], 71), 0),
        "grad_out": centred(splits[2], (TOKENS, HEADS * HD), (max(TOKENS // 1024, 1)) ** -0.5, 3.0, ((0, 32),)),
        "inputs": centred(splits[3], (TOKENS, D), 1.0, 6.0, ((0, 32),)),
        "old_owner": draw_old_owner(jax.random.fold_in(splits[9], 71), 0),
        "new_owner": draw_new_owner(jax.random.fold_in(splits[9], 71), 0),
        "param_old": centred(splits[6], (BROWS, N_SHARD * OLD_CAP, KV * HD), 0.05, 0.75, ((0, 8), (1, 4)), jnp.float32),
        "first_old": centred(splits[7], (BROWS, N_SHARD * OLD_CAP, KV * HD), 1.0, 6.0, ((0, 8), (1, 4)), jnp.float32),
        "second_old": jnp.clip(jnp.exp(math.log(20.0) - 3.6888795 * jax.random.uniform(splits[8], (BROWS, N_SHARD * OLD_CAP, KV * HD), jnp.float32) ** shard_levels(splits[8], (BROWS, N_SHARD * OLD_CAP, KV * HD), ((0, 8), (1, 4)), -0.2, 0.2)), 0.5, 20.0),
    }


beta_first = 0.9
beta_second = 0.95
learning_rate = 0.02
decay_rate = 0.1
epsilon = 1e-08

def owner_ranks(owner, owners):
    onehot = (owner[:, None] == jnp.arange(owners, dtype=jnp.int32)[None, :]).astype(jnp.int32)
    running = jnp.cumsum(onehot, axis=0)
    return (lax.optimization_barrier(jnp.sum(running * onehot, axis=1)) - 1).astype(jnp.int32)

def adamw(param, first, second, gradient):
    first = beta_first * first + (1.0 - beta_first) * gradient
    second = beta_second * second + (1.0 - beta_second) * gradient * gradient
    first_hat = first / (1.0 - beta_first ** STEP)
    second_hat = second / (1.0 - beta_second ** STEP)
    param = param - learning_rate * (first_hat / (jnp.sqrt(second_hat) + epsilon) + decay_rate * param)
    return (param, first, second)

def group_values(triple):
    query_block, key_block, cotangent = triple
    length = key_block.shape[0]
    scores = jnp.einsum('htd,ud->htu', query_block.astype(jnp.float32), key_block.astype(jnp.float32)) * HD ** (-0.5)
    allowed = jnp.arange(length)[None, :] <= jnp.arange(length)[:, None]
    scores = jnp.where(allowed[None], scores, -jnp.inf)
    highest = lax.optimization_barrier(jnp.max(scores, axis=-1, keepdims=True))
    weights = jnp.exp(scores - highest)
    probs = (weights / lax.optimization_barrier(jnp.sum(weights, axis=-1, keepdims=True))).astype(jnp.bfloat16)
    summed = jnp.einsum('htu,htd->ud', probs.astype(jnp.float32), cotangent.astype(jnp.float32))
    return summed.astype(jnp.bfloat16)

def sequence_values(triple):
    return lax.map(group_values, triple)

def reference(queries, keys, grad_out, inputs, old_owner, new_owner, param_old, first_old, second_old):
    seq_count = TOKENS // LENGTH
    query_groups = queries.reshape(seq_count, LENGTH, KV, GRP, HD).transpose(0, 2, 3, 1, 4)
    cotangent_groups = grad_out.reshape(seq_count, LENGTH, KV, GRP, HD).transpose(0, 2, 3, 1, 4)
    key_groups = keys.reshape(seq_count, LENGTH, KV, HD).transpose(0, 2, 1, 3)
    values = lax.map(sequence_values, (query_groups, key_groups, cotangent_groups))
    values = values.transpose(0, 2, 1, 3).reshape(TOKENS, KV * HD)
    gradient = lax.dot_general(inputs, values, (((0,), (0,)), ((), ())), preferred_element_type=jnp.float32)
    gradient = gradient.reshape(BLOCKS, BROWS, KV * HD).transpose(1, 0, 2)
    old_slot = (old_owner * OLD_CAP + owner_ranks(old_owner, N_SHARD)).astype(jnp.int32)
    param = jnp.take(param_old, old_slot, axis=1)
    first = jnp.take(first_old, old_slot, axis=1)
    second = jnp.take(second_old, old_slot, axis=1)
    param, first, second = adamw(param, first, second, gradient)
    new_slot = (new_owner * NEW_CAP + owner_ranks(new_owner, N_SHARD)).astype(jnp.int32)
    placing = jnp.argsort(new_slot).astype(jnp.int32)
    param_new = jnp.take(param, placing, axis=1)
    first_new = jnp.take(first, placing, axis=1)
    second_new = jnp.take(second, placing, axis=1)
    weights = param.astype(jnp.bfloat16)
    return (param_new, first_new, second_new, weights)
```

```python
import functools

import jax
import jax.numpy as jnp
from jax import lax
from jax.experimental import pallas as pl
from jax.experimental.pallas import tpu as pltpu
from jax.sharding import PartitionSpec as P

KV = 4
HD = 128
GRP = 8
STEP = 1000

beta_first = 0.9
beta_second = 0.95
learning_rate = 0.02
decay_rate = 0.1
epsilon = 1e-08


def owner_ranks(owner, owners):
    onehot = (owner[:, None] == jnp.arange(owners, dtype=jnp.int32)[None, :]).astype(jnp.int32)
    running = jnp.cumsum(onehot, axis=0)
    return jnp.sum(running * onehot, axis=1) - 1


def adamw(param, first, second, gradient):
    first = beta_first * first + (1.0 - beta_first) * gradient
    second = beta_second * second + (1.0 - beta_second) * gradient * gradient
    first_hat = first / (1.0 - beta_first**STEP)
    second_hat = second / (1.0 - beta_second**STEP)
    param = param - learning_rate * (
        first_hat / (jnp.sqrt(second_hat) + epsilon) + decay_rate * param
    )
    return (param, first, second)


def value_kernel(where_ref, q_ref, k_ref, g_ref, o_ref):
    me = where_ref[0]
    rows = q_ref.shape[0]
    length = k_ref.shape[0]
    row = lax.broadcasted_iota(jnp.int32, (rows, length), 0)
    col = lax.broadcasted_iota(jnp.int32, (rows, length), 1)
    allowed = col <= jnp.where(col < rows, row, (me + 1) * rows - 1)
    keys = k_ref[...]
    total = jnp.zeros((length, HD), jnp.float32)
    for h in range(GRP):
        span = slice(h * HD, (h + 1) * HD)
        scores = lax.dot_general(
            q_ref[:, span], keys, (((1,), (1,)), ((), ())), preferred_element_type=jnp.float32
        ) * HD ** (-0.5)
        scores = jnp.where(allowed, scores, -jnp.inf)
        highest = jnp.max(scores, axis=-1, keepdims=True)
        weights = jnp.exp(scores - highest)
        probs = (weights / jnp.sum(weights, axis=-1, keepdims=True)).astype(jnp.bfloat16)
        total = total + lax.dot_general(
            probs, g_ref[:, span], (((0,), (0,)), ((), ())), preferred_element_type=jnp.float32
        )
    o_ref[...] = total


def value_terms(me, queries, keys_all, grad_out):
    rows = queries.shape[0]
    length = keys_all.shape[0]
    return pl.pallas_call(
        value_kernel,
        grid=(KV,),
        out_shape=jax.ShapeDtypeStruct((length, KV * HD), jnp.float32),
        in_specs=[
            pl.BlockSpec(memory_space=pltpu.SMEM),
            pl.BlockSpec((rows, GRP * HD), lambda g: (0, g)),
            pl.BlockSpec((length, HD), lambda g: (0, g)),
            pl.BlockSpec((rows, GRP * HD), lambda g: (0, g)),
        ],
        out_specs=pl.BlockSpec((length, HD), lambda g: (0, g)),
        cost_estimate=pl.CostEstimate(
            flops=4 * rows * length * HD * GRP * KV, bytes_accessed=4 << 20, transcendentals=0
        ),
    )(me[None], queries, keys_all, grad_out)


def pick_kernel(block_ref, x_ref, o_ref, p_ref):
    width = HD
    count = o_ref.shape[1] // width

    @pl.loop(0, count)
    def _(i):
        into = pl.ds(pl.multiple_of(i * width, width), width)
        o_ref[:, into] = x_ref[:, pl.ds(pl.multiple_of(block_ref[0, i] * width, width), width)]
        p_ref[:, into] = x_ref[:, pl.ds(pl.multiple_of(block_ref[1, i] * width, width), width)]


def pick(blocks, inputs):
    rows, wide = inputs.shape
    half = jax.ShapeDtypeStruct((rows, wide // 2), inputs.dtype)
    return pl.pallas_call(
        pick_kernel,
        out_shape=(half, half),
        in_specs=[
            pl.BlockSpec(memory_space=pltpu.SMEM),
            pl.BlockSpec(memory_space=pltpu.VMEM),
        ],
        out_specs=(pl.BlockSpec(memory_space=pltpu.VMEM),) * 2,
        cost_estimate=pl.CostEstimate(flops=0, bytes_accessed=4 << 20, transcendentals=0),
    )(blocks, inputs)


def swap(x, axis, size, bit):
    return lax.ppermute(x, axis, [(i, i ^ bit) for i in range(size)])


def halve(x, axis, bit_value):
    mine = lax.dynamic_index_in_dim(x, bit_value, axis, keepdims=False)
    other = lax.dynamic_index_in_dim(x, 1 - bit_value, axis, keepdims=False)
    return mine, other


def spread(onehot, state):
    return jnp.einsum(
        "ns,rsc->rnc",
        onehot.astype(state.dtype),
        state,
        precision=lax.Precision.HIGHEST if state.dtype == jnp.float32 else None,
        preferred_element_type=state.dtype,
    )


def moved_state(state, source_owner, source_rank, me, shards, sources, new_capacity):
    old_capacity = state.shape[1]
    rank_hot = source_rank[:, None] == jnp.arange(old_capacity)[None, :]
    mine = spread(rank_hot & (source_owner == me)[:, None], state)

    def my_part(x, first_shard, count):
        at = jnp.clip(me - first_shard, 0, count - 1) * new_capacity
        part = lax.dynamic_slice_in_dim(x, at, new_capacity, axis=1)
        inside = (me >= first_shard) & (me < first_shard + count)
        return jnp.where(inside, part, jnp.zeros_like(part))

    result = my_part(mine, 0, shards)

    def chain(route):
        out = jnp.zeros_like(result)
        come = None
        for step, (sender, receiver, low, high) in enumerate(route):
            count = high - low
            if step == 0 and old_capacity < count * new_capacity:
                raw = lax.ppermute(state, "shard", [(sender, receiver)])
                come = spread(
                    (rank_hot & (source_owner == sender)[:, None])[
                        low * new_capacity : high * new_capacity
                    ],
                    raw,
                )
            else:
                pay = mine[:, low * new_capacity : high * new_capacity]
                if come is not None:
                    skip = (low - before) * new_capacity
                    pay = pay + come[:, skip : skip + count * new_capacity]
                come = lax.ppermute(pay, "shard", [(sender, receiver)])
            before = low
            here = receiver - low
            part = come[:, here * new_capacity : (here + 1) * new_capacity]
            out = out + jnp.where(me == receiver, part, jnp.zeros_like(part))
        return out

    right = chain([(l, l + 1, l + 1, shards) for l in range(shards - 1)])
    left = chain([(l, l - 1, 0, l) for l in range(sources - 1, 0, -1)])
    return result + right + left


def local(queries, keys, grad_out, inputs, old_owner, new_owner, param_old, first_old, second_old):
    shards = lax.axis_size("shard")
    replicas = lax.axis_size("rep")
    me = lax.axis_index("shard")
    rep = lax.axis_index("rep")
    rows = queries.shape[0]
    blocks = old_owner.shape[0]
    block_rows = inputs.shape[1] // blocks
    own_rows = block_rows // replicas
    new_capacity = blocks // shards
    columns = KV * HD
    sources = shards - shards // 4
    bf16 = jnp.bfloat16

    chunks = [keys]
    for k in range(1, shards):
        chunks.append(lax.ppermute(keys, "shard", [(s, s + k) for s in range(shards - k)]))

    new_slot = new_owner * new_capacity + owner_ranks(new_owner, shards)
    match = new_slot[None, :] == jnp.arange(blocks, dtype=jnp.int32)[:, None]

    def by_slot(table):
        return jnp.sum(jnp.where(match, table[None, :], 0), axis=1)

    new_block = by_slot(jnp.arange(blocks, dtype=jnp.int32))
    source_owner = by_slot(old_owner)
    source_rank = by_slot(owner_ranks(old_owner, shards))

    parity = me % 2
    halves = new_block.reshape(shards // 2, 2, new_capacity).transpose(1, 0, 2).reshape(2, -1)
    mine_first = jnp.where(parity == 0, halves, halves[::-1])
    kept, sent = pick(mine_first, inputs)
    arrived = swap(sent, "shard", shards, 1)

    moved = [
        moved_state(x, source_owner, source_rank, me, shards, sources, new_capacity)
        for x in (first_old.astype(bf16), second_old.astype(bf16), param_old)
    ]
    first, second, param = (x.astype(jnp.float32) for x in moved)

    part = value_terms(me, queries, jnp.concatenate(chunks, axis=0), grad_out)
    values = part[:rows]
    for k in range(1, shards):
        values = values + lax.ppermute(
            part[k * rows : (k + 1) * rows], "shard", [(s, s - k) for s in range(k, shards)]
        )
    values = values.astype(bf16)
    values_pair = swap(values, "shard", shards, 1)

    contract = (((0,), (0,)), ((), ()))
    product = lax.dot_general(
        jnp.concatenate([kept, arrived], axis=0),
        jnp.concatenate([values, values_pair], axis=0),
        contract,
        preferred_element_type=jnp.float32,
    )
    bits = [1 << n for n in range(replicas.bit_length() - 1)]
    split = tuple(2 for _ in bits)
    product = product.reshape((-1,) + split + (own_rows, columns))

    def scatter(x, order):
        left = sorted(order, reverse=True)
        for bit in order:
            mine, other = halve(x, 1 + left.index(bit), (rep // bit) % 2)
            x = mine + swap(other.astype(bf16), "rep", replicas, bit).astype(jnp.float32)
            left.remove(bit)
        return x

    mine, other = halve(product, len(bits), rep % 2)
    product = mine + swap(other.astype(bf16), "rep", replicas, 1).astype(jnp.float32)
    product = product.reshape((2, -1) + product.shape[1:])
    a = scatter(product[0], bits[1:])
    b = scatter(product[1], bits[:0:-1])
    gradient = jnp.concatenate([a, b], axis=0).reshape(
        shards // 2, new_capacity, own_rows, columns
    )
    pair = me // 2
    total = lax.dynamic_index_in_dim(gradient, pair, 0, keepdims=False)
    for k in range(1, shards // 2):
        out = lax.dynamic_index_in_dim(gradient, (pair + k) % (shards // 2), 0, keepdims=False)
        total = total + lax.ppermute(
            out.astype(bf16), "shard", [(s, (s + 2 * k) % shards) for s in range(shards)]
        ).astype(jnp.float32)
    gradient = total.transpose(1, 0, 2)

    param_new, first_new, second_new = adamw(param, first, second, gradient)
    working = param_new.astype(bf16)
    every = [working]
    for k in range(1, shards):
        every.append(
            lax.ppermute(working, "shard", [(s, (s + k) % shards) for s in range(shards)])
        )
    stacked = jnp.concatenate(every, axis=1)
    at = ((me - new_slot // new_capacity) % shards) * new_capacity + new_slot % new_capacity
    weights = spread(at[:, None] == jnp.arange(blocks)[None, :], stacked)
    return (param_new, first_new, second_new, weights)


def table_kernel(old_ref, new_ref, tab_ref, *, capacity):
    count = old_ref.shape[1]
    sub = lax.broadcasted_iota(jnp.int32, (count, count), 0)
    lane = lax.broadcasted_iota(jnp.int32, (count, count), 1)

    def ranks(ref):
        across = jnp.broadcast_to(ref[...], (count, count))
        down = jnp.sum(jnp.where(sub == lane, across, 0), axis=1, keepdims=True)
        same = across == down
        below = jnp.sum(jnp.where(same & (lane < sub), 1, 0), axis=1, keepdims=True)
        before = jnp.sum(jnp.where(same & (sub < lane), 1, 0), axis=0, keepdims=True)
        return down, below, before

    old, old_rank, _ = ranks(old_ref)
    new, new_rank, new_rank_row = ranks(new_ref)
    hit = new * capacity + new_rank == lane
    for at, table in enumerate((sub, old, old_rank)):
        tab_ref[at : at + 1, :] = jnp.sum(jnp.where(hit, table, 0), axis=0, keepdims=True)
    tab_ref[3:4, :] = new_ref[...] * capacity + new_rank_row


def fused_kernel(
    tab, q_h, key_h, g_h, x_h, p_h, f_h, s_h,
    pn_h, fn_h, sn_h, wall_h,
    q_ref, g_ref, x_ref, state, kbuf, part, vo, v_in, vals, xs, xt, xo,
    st_own, raw_a0, raw_a1, raw_a2, raw_a3, raw_b0, raw_b1, raw_b2, raw_b3,
    r_out, a_in, l_out, l_in, d_out, d_in, settled,
    gbuf, pass_out, pass_in, mid_out, mid_in, fin_out, fin_in, grad, tmp, outv, wall,
    load_sem, k_sem, x_sem, xl_sem, v_sem, va_sem, raw_sem, st_sem,
    pass_sem, mid_sem, fin_sem, w_sem, out_sem, wo_sem,
):
    bf16, f32 = jnp.bfloat16, jnp.float32
    me, rep = lax.axis_index("shard"), lax.axis_index("rep")
    shards = kbuf.shape[1]
    rows = key_h.shape[0]
    length = shards * rows
    cap = pn_h.shape[1]
    blocks = xs.shape[1]
    own_rows = xs.shape[2]
    replicas = xs.shape[0]
    slots = cap * own_rows
    pieces = x_sem.shape[0]
    sources = shards - 1
    raw_a = (raw_a0, raw_a1, raw_a2, raw_a3)
    raw_b = (raw_b0, raw_b1, raw_b2, raw_b3)
    bits = (rep % 2, (rep // 2) % 2, rep // 4)
    has_left, has_right = me > 0, me < shards - 1
    edge = (me == 0) | (me == shards - 1)
    inner = (me > 0) & (me < shards - 1)
    pair = me + 1 - 2 * (me % 2)
    mid = shards - 1 - me
    side = me // 2
    near = 2 - side
    far = 3 - 3 * side
    left, right = (rep, me - 1), (rep, me + 1)

    def peer(k):
        return sum(
            (1 << n) * (bit + ((k >> n) & 1) * (1 - 2 * bit)) for n, bit in enumerate(bits)
        )

    def send(src, dst, sem, target):
        return pltpu.make_async_remote_copy(
            src_ref=src, dst_ref=dst, send_sem=sem.at[0], recv_sem=sem.at[1],
            device_id=target, device_id_type=pl.DeviceIdType.MESH,
        )

    def cols(g):
        return pl.ds(g * HD, HD)

    def key_load(g):
        return pltpu.make_async_copy(key_h.at[:, cols(g)], kbuf.at[g, 0], load_sem.at[g])

    wide = x_h.shape[1] // pieces

    def x_load(p):
        span = pl.ds(p * wide, wide)
        return pltpu.make_async_copy(x_h.at[:, span], x_ref.at[:, span], load_sem.at[KV + p])

    late = KV + pieces
    q_load = pltpu.make_async_copy(q_h, q_ref, load_sem.at[late])
    g_load = pltpu.make_async_copy(g_h, g_ref, load_sem.at[late + 1])
    s_loads = [
        pltpu.make_async_copy(src, state.at[i], load_sem.at[late + 2 + i])
        for i, src in enumerate((p_h, f_h, s_h))
    ]
    for g in range(KV):
        key_load(g).start()
    for p in range(pieces):
        x_load(p).start()
    q_load.start()
    g_load.start()
    for copy in s_loads:
        copy.start()

    barrier = pltpu.get_barrier_semaphore()

    def greet(target):
        pl.semaphore_signal(barrier, inc=1, device_id=target, device_id_type=pl.DeviceIdType.MESH)

    for k in range(1, replicas):
        greet((peer(k), me))
    pl.when(has_left)(lambda: greet(left))
    pl.when(has_right)(lambda: greet(right))
    for g in range(KV):
        key_load(g).wait()
    pl.semaphore_wait(barrier, replicas + jnp.where(inner, 1, 0))

    def key_copy(g, j):
        return send(kbuf.at[g, j], kbuf.at[g, j + 1], k_sem.at[g, j], right)

    for g in range(KV):
        pl.when(has_right)(lambda g=g: key_copy(g, 0).start())

    group = blocks // pieces

    def x_copy(p, k):
        span = pl.ds(p * group, group)
        return send(
            xs.at[peer(k), span],
            xt.at[span, :, pl.ds(pl.multiple_of(rep * rows, rows), rows)],
            x_sem.at[p, k],
            (peer(k), me),
        )

    def x_keep(p):
        span = pl.ds(p * group, group)
        return pltpu.make_async_copy(
            xs.at[rep, span],
            xt.at[span, :, pl.ds(pl.multiple_of(rep * rows, rows), rows)],
            xl_sem.at[p],
        )

    for p in range(pieces):
        x_load(p).wait()

        @pl.loop(p * group, (p + 1) * group)
        def _(b):
            block = x_ref[:, pl.ds(pl.multiple_of(b * HD, HD), HD)].T
            xs[:, b] = block.reshape(replicas, own_rows, rows)

        for k in (2, 4, 6, 3, 5, 7, 1):
            x_copy(p, k).start()
        x_keep(p).start()

    for copy in s_loads:
        copy.wait()

    @pl.loop(0, st_own.shape[1])
    def _(s):
        for g in range(KV):
            for i in range(3):
                st_own[g, s, i] = state[i, s, :, g * HD : (g + 1) * HD].astype(bf16)

    def raw_right(g):
        return send(st_own.at[g], raw_a[g], raw_sem.at[g, 0], right)

    def raw_left(g):
        return send(st_own.at[g], raw_b[g], raw_sem.at[g, 1], left)

    def send_left(g):
        pl.when(me == sources - 1)(lambda: raw_left(g).start())

    for g in range(KV):
        pl.when(me == 0)(lambda g=g: raw_right(g).start())
    send_left(0)

    for j in range(1, shards):
        for g in range(KV):
            @pl.when((me >= j) & has_right)
            def _(g=g, j=j):
                key_copy(g, j - 1).wait_recv()
                if j < shards - 1:
                    key_copy(g, j).start()

            @pl.when(me < j)
            def _(g=g, j=j):
                kbuf[g, j] = jnp.zeros(kbuf.shape[2:], kbuf.dtype)

    def v_copy(g, c):
        return send(vo.at[g, c], v_in.at[g, c], v_sem.at[g, c], left)

    def va_copy(g, k):
        return send(vals.at[g, rep], vals.at[g, rep], va_sem.at[g, k], (peer(k), me))

    def va_relay(g, k):
        return send(vals.at[g, peer(k)], vals.at[g, peer(k)], va_sem.at[g, k + 1], (peer(1), me))

    def finish(g, value):
        vals[g, rep] = value.astype(bf16)
        for k in (6, 2, 4, 1):
            va_copy(g, k).start()

    q_load.wait()
    g_load.wait()
    row = lax.broadcasted_iota(jnp.int32, (rows, length), 0)
    col = lax.broadcasted_iota(jnp.int32, (rows, length), 1)
    allowed = col <= jnp.where(col < rows, row, (me + 1) * rows - 1)

    @pl.loop(0, KV)
    def _(g):
        @pl.when(me == shards - 1)
        def _():
            for j in range(shards - 1):
                key_copy(g, j).wait_recv()

        keys = kbuf[g].reshape(length, HD)
        total = jnp.zeros((length, HD), f32)
        for h in range(GRP):
            span = pl.ds(pl.multiple_of(g * (GRP * HD) + h * HD, HD), HD)
            scores = lax.dot_general(
                q_ref[:, span], keys, (((1,), (1,)), ((), ())), preferred_element_type=f32
            ) * HD ** (-0.5)
            scores = jnp.where(allowed, scores, -jnp.inf)
            highest = jnp.max(scores, axis=-1, keepdims=True)
            weights = jnp.exp(scores - highest)
            probs = (weights / jnp.sum(weights, axis=-1, keepdims=True)).astype(bf16)
            total = total + lax.dot_general(
                probs, g_ref[:, span], (((0,), (0,)), ((), ())), preferred_element_type=f32
            )
        part[g] = total.reshape(shards, rows, HD)

        @pl.when(me == shards - 1)
        def _():
            for c in range(shards - 1):
                vo[g, c] = part[g, shards - 1 - c]
                v_copy(g, c).start()
            finish(g, part[g, 0])

    def chain(g):
        for c in range(shards - 1):
            @pl.when((me > c) & has_right)
            def _(c=c):
                v_copy(g, c).wait_recv()
                vo[g, c] = part[g, me - c] + v_in[g, c]
                v_copy(g, c).start()

            @pl.when(me == c)
            def _(c=c):
                v_copy(g, c).wait_recv()
                finish(g, part[g, 0] + v_in[g, c])

    def r_copy(g, i):
        return send(r_out.at[g, i], a_in.at[g, i], st_sem.at[g, i], right)

    def l_copy(g):
        return send(l_out.at[g], l_in.at[g], st_sem.at[g, 2], left)

    def d_copy(g):
        return send(d_out.at[g], d_in.at[g], st_sem.at[g, 3], right)

    def choose(g, owner, first, out, other):
        @pl.loop(0, cap)
        def _(j):
            s = first * cap + j
            at = tab[2, s]
            out[j] = jnp.where(tab[1, s] == owner, st_own[g, at], other(j, at))

    def route_right(g):
        @pl.when(me == 1)
        def _():
            raw_right(g).wait_recv()
            for i, first in enumerate((3, 2)):
                choose(g, 1, first, r_out.at[g, i], lambda j, at: raw_a[g][at])
                r_copy(g, i).start()

    def route_left(g):
        @pl.when(me == 1)
        def _():
            raw_left(g).wait_recv()
            choose(g, 1, 0, l_out.at[g], lambda j, at: raw_b[g][at])
            l_copy(g).start()

    def route_last(g):
        @pl.when(me == 2)
        def _():
            r_copy(g, 0).wait_recv()
            choose(g, 2, 3, d_out.at[g], lambda j, at: a_in[g, 0, j])
            d_copy(g).start()

    def settle(g):
        def take(other):
            @pl.loop(0, cap)
            def _(j):
                s = me * cap + j
                at = tab[2, s]
                mine = tab[1, s] == me
                moved = other(j, s, at)
                for i in range(3):
                    settled[i, j] = jnp.where(
                        mine, state[i, at, :, g * HD : (g + 1) * HD], moved[i].astype(f32)
                    )

        @pl.when(me == 0)
        def _():
            l_copy(g).wait_recv()
            take(lambda j, s, at: l_in[g, j])

        @pl.when(me == 1)
        def _():
            take(lambda j, s, at: jnp.where(tab[1, s] == 0, raw_a[g][at], raw_b[g][at]))

        @pl.when(me == 2)
        def _():
            r_copy(g, 1).wait_recv()
            take(lambda j, s, at: a_in[g, 1, j])

        @pl.when(me == 3)
        def _():
            d_copy(g).wait_recv()
            take(lambda j, s, at: d_in[g, j])

    def pass_copy(g, i):
        return send(pass_out.at[g, i], pass_in.at[g, i], pass_sem.at[g, i], (rep, pair))

    def mid_copy(g, i):
        return send(mid_out.at[g, i], mid_in.at[g, i], mid_sem.at[g, i], (rep, mid))

    def fin_copy(g):
        return send(fin_out.at[g], fin_in.at[g], fin_sem.at[g], (rep, pair))

    def arrange():
        for p in range(pieces):
            for k in range(1, replicas):
                x_copy(p, k).wait_recv()
            x_keep(p).wait()

        @pl.loop(0, blocks)
        def _(s):
            xo[s] = xt[tab[0, s]]

    def product(g):
        for k in (2, 4, 6):
            va_copy(g, k).wait_recv()
            va_relay(g, k).start()
        va_copy(g, 1).wait_recv()
        for k in (2, 4, 6):
            va_relay(g, k).wait_recv()
        value = vals[g].reshape(replicas * rows, HD)

        @pl.loop(0, shards)
        def _(o):
            block = xo[pl.ds(o * cap, cap)].reshape(slots, replicas * rows)
            gbuf[g, o] = jnp.dot(block, value, preferred_element_type=f32)

        @pl.when(edge)
        def _():
            for i, to in enumerate((far, near)):
                pass_out[g, i] = gbuf[g, to].astype(bf16)
                pass_copy(g, i).start()
            fin_out[g] = gbuf[g, pair]
            fin_copy(g).start()

    def cross(g):
        @pl.when(inner)
        def _():
            for i, to in enumerate((far, near)):
                pass_copy(g, i).wait_recv()
                mid_out[g, i] = (gbuf[g, to] + pass_in[g, i].astype(f32)).astype(bf16)
                mid_copy(g, i).start()

    def back(g):
        @pl.when(inner)
        def _():
            mid_copy(g, 0).wait_recv()
            fin_out[g] = gbuf[g, pair] + mid_in[g, 0].astype(f32)
            fin_copy(g).start()

    def w_copy(g, t, direction):
        origin = (me - t, me + t)[direction]
        ref = wall.at[g, origin]
        return send(ref, ref, w_sem.at[g, t, direction], (right, left)[direction])

    def w_out(g, origin):
        at = pl.ds(pl.multiple_of(origin * cap, cap), cap)
        return pltpu.make_async_copy(wall.at[g, origin], wall_h.at[:, at, cols(g)], wo_sem.at[g, origin])

    def state_out(g, i):
        return pltpu.make_async_copy(
            outv.at[i, g], (pn_h, fn_h, sn_h)[i].at[:, :, cols(g)], out_sem.at[g, i]
        )

    def update(g):
        settle(g)
        fin_copy(g).wait_recv()

        @pl.when(edge)
        def _():
            grad[...] = gbuf[g, me] + fin_in[g]

        @pl.when(inner)
        def _():
            mid_copy(g, 1).wait_recv()
            grad[...] = gbuf[g, me] + fin_in[g] + mid_in[g, 1].astype(f32)

        @pl.loop(0, cap)
        def _(j):
            at = pl.ds(pl.multiple_of(j * own_rows, own_rows), own_rows)
            new = adamw(settled[0, j], settled[1, j], settled[2, j], grad[at, :])
            for i in range(3):
                tmp[i, at, :] = new[i]

        for r in range(own_rows):
            param = tmp[0, pl.ds(r, cap, stride=own_rows), :]
            outv[0, g, r] = param
            wall[g, me, r] = param.astype(bf16)
        pl.when(has_right)(lambda: w_copy(g, 0, 0).start())
        pl.when(has_left)(lambda: w_copy(g, 0, 1).start())
        for r in range(own_rows):
            for i in (1, 2):
                outv[i, g, r] = tmp[i, pl.ds(r, cap, stride=own_rows), :]
        w_out(g, me).start()
        for i in range(3):
            state_out(g, i).start()

    def gather(g, t):
        @pl.when(me >= t)
        def _():
            arrived = wall.at[g, me - t]
            send(arrived, arrived, w_sem.at[g, t - 1, 0], right).wait_recv()
            if t < shards - 1:
                pl.when(has_right)(lambda: w_copy(g, t, 0).start())
            w_out(g, me - t).start()

        @pl.when(me + t < shards)
        def _():
            arrived = wall.at[g, me + t]
            send(arrived, arrived, w_sem.at[g, t - 1, 1], left).wait_recv()
            if t < shards - 1:
                pl.when(has_left)(lambda: w_copy(g, t, 1).start())
            w_out(g, me + t).start()

    steps = [
        (route_right, 0), (chain, 0), (chain, 1), (send_left, 1), (route_right, 1), (route_left, 0),
        (chain, 2), (chain, 3), (send_left, 2), (route_left, 1), (route_last, 0), (arrange,),
        (product, 0), (route_right, 2), (cross, 0), (product, 1), (back, 0), (cross, 1),
        (send_left, 3), (route_last, 1), (route_left, 2), (product, 2), (back, 1), (cross, 2),
        (route_right, 3), (update, 0), (product, 3), (back, 2), (cross, 3),
        (route_last, 2), (route_left, 3), (gather, 0, 1), (update, 1), (back, 3),
        (gather, 0, 2), (gather, 1, 1), (route_last, 3), (update, 2),
        (gather, 0, 3), (gather, 1, 2), (gather, 2, 1), (update, 3),
        (gather, 1, 3), (gather, 2, 2), (gather, 3, 1), (gather, 2, 3), (gather, 3, 2), (gather, 3, 3),
    ]
    for step, *at in steps:
        step(*at)

    for g in range(KV):
        for j in range(shards - 1):
            pl.when(has_right & (me >= j))(lambda g=g, j=j: key_copy(g, j).wait_send())
        for c in range(shards - 1):
            pl.when(me > c)(lambda g=g, c=c: v_copy(g, c).wait_send())
        for k in (6, 2, 4, 1):
            va_copy(g, k).wait_send()
        for k in (2, 4, 6):
            va_relay(g, k).wait_send()

        @pl.when(me == 0)
        def _(g=g):
            raw_right(g).wait_send()

        @pl.when(me == 1)
        def _(g=g):
            r_copy(g, 0).wait_send()
            r_copy(g, 1).wait_send()
            l_copy(g).wait_send()

        @pl.when(me == 2)
        def _(g=g):
            raw_left(g).wait_send()
            d_copy(g).wait_send()

        @pl.when(edge)
        def _(g=g):
            for i in range(2):
                pass_copy(g, i).wait_send()

        @pl.when(inner)
        def _(g=g):
            for i in range(2):
                mid_copy(g, i).wait_send()

        fin_copy(g).wait_send()
        for t in range(shards - 1):
            pl.when(has_right & (me >= t))(lambda g=g, t=t: w_copy(g, t, 0).wait_send())
            pl.when(has_left & (me + t < shards))(lambda g=g, t=t: w_copy(g, t, 1).wait_send())
        for o in range(shards):
            w_out(g, o).wait()
        for i in range(3):
            state_out(g, i).wait()
    for p in range(pieces):
        for k in range(1, replicas):
            x_copy(p, k).wait_send()


def fused(queries, keys, grad_out, inputs, old_owner, new_owner, param_old, first_old, second_old):
    shards = lax.axis_size("shard")
    replicas = lax.axis_size("rep")
    rows = queries.shape[0]
    blocks = old_owner.shape[0]
    own_rows = inputs.shape[1] // blocks // replicas
    cap = blocks // shards
    width = KV * HD
    old_cap = param_old.shape[1]
    bf16, f32 = jnp.bfloat16, jnp.float32
    pieces = 4

    tab = pl.pallas_call(
        functools.partial(table_kernel, capacity=cap),
        out_shape=jax.ShapeDtypeStruct((4, blocks), jnp.int32),
    )(old_owner[None], new_owner[None])

    slot = jax.ShapeDtypeStruct((own_rows, cap, width), f32)
    V = pltpu.VMEM
    tokens = replicas * rows
    slots = cap * own_rows

    def state(*count):
        return V((*count, 3, own_rows, HD), bf16)

    def dma(*shape):
        return pltpu.SemaphoreType.DMA(shape)

    outs = pl.pallas_call(
        fused_kernel,
        out_shape=(slot, slot, slot, jax.ShapeDtypeStruct((own_rows, blocks, width), bf16)),
        in_specs=[pl.BlockSpec(memory_space=pltpu.SMEM)] + [pl.BlockSpec(memory_space=pl.ANY)] * 7,
        out_specs=(pl.BlockSpec(memory_space=pl.ANY),) * 4,
        scratch_shapes=[
            V(queries.shape, bf16), V(grad_out.shape, bf16), V(inputs.shape, bf16),
            V((3, old_cap, own_rows, width), f32),
            V((KV, shards, rows, HD), bf16),
            V((KV, shards, rows, HD), f32),
            V((KV, shards - 1, rows, HD), f32), V((KV, shards - 1, rows, HD), f32),
            V((KV, replicas, rows, HD), bf16),
            V((replicas, blocks, own_rows, rows), bf16),
            V((blocks, own_rows, tokens), bf16), V((blocks, own_rows, tokens), bf16),
            state(KV, old_cap),
            *[state(old_cap)] * 8,
            state(KV, 2, cap), state(KV, 2, cap),
            state(KV, cap), state(KV, cap), state(KV, cap), state(KV, cap),
            V((3, cap, own_rows, HD), f32),
            V((KV, shards, slots, HD), f32),
            *[V((KV, 2, slots, HD), bf16)] * 4,
            V((KV, slots, HD), f32), V((KV, slots, HD), f32),
            V((slots, HD), f32), V((3, slots, HD), f32),
            V((3, KV, own_rows, cap, HD), f32),
            V((KV, shards, own_rows, cap, HD), bf16),
            dma(KV + pieces + 5), dma(KV, shards - 1, 2), dma(pieces, replicas, 2), dma(pieces),
            dma(KV, shards - 1, 2), dma(KV, replicas, 2), dma(KV, 2, 2), dma(KV, 4, 2),
            dma(KV, 2, 2), dma(KV, 2, 2), dma(KV, 2), dma(KV, shards - 1, 2, 2),
            dma(KV, 3), dma(KV, shards),
        ],
        compiler_params=pltpu.CompilerParams(
            collective_id=0, has_side_effects=True, vmem_limit_bytes=63 << 20
        ),
    )(
        tab, queries, keys, grad_out, inputs,
        *[jnp.transpose(x, (1, 0, 2)) for x in (param_old, first_old, second_old)],
    )
    weights = spread(tab[3][:, None] == jnp.arange(blocks)[None, :], outs[3])
    return tuple(outs[:3]) + (weights,)


def solution(mesh):
    placed = (
        P(("rep", "shard"), None),
        P(("rep", "shard"), None),
        P(("rep", "shard"), None),
        P(("rep", "shard"), None),
        P(),
        P(),
        P("rep", "shard", None),
        P("rep", "shard", None),
        P("rep", "shard", None),
    )
    small = mesh.shape["shard"] == 4 and mesh.shape["rep"] == 8
    return jax.shard_map(
        fused if small else local,
        mesh=mesh,
        in_specs=placed,
        out_specs=(
            P("rep", "shard", None),
            P("rep", "shard", None),
            P("rep", "shard", None),
            P("rep", None, None),
        ),
        check_vma=False,
    )
```

```python
import functools

import jax
import jax.numpy as jnp
from jax import lax
from jax.experimental import pallas as pl
from jax.experimental.pallas import tpu as pltpu
from jax.sharding import PartitionSpec as P

KV = 4
HD = 128
GRP = 8
STEP = 1000

beta_first = 0.9
beta_second = 0.95
learning_rate = 0.02
decay_rate = 0.1
epsilon = 1e-08


def owner_ranks(owner, owners):
    onehot = (owner[:, None] == jnp.arange(owners, dtype=jnp.int32)[None, :]).astype(jnp.int32)
    running = jnp.cumsum(onehot, axis=0)
    return jnp.sum(running * onehot, axis=1) - 1


def adamw(param, first, second, gradient):
    first = beta_first * first + (1.0 - beta_first) * gradient
    second = beta_second * second + (1.0 - beta_second) * gradient * gradient
    first_hat = first / (1.0 - beta_first**STEP)
    second_hat = second / (1.0 - beta_second**STEP)
    param = param - learning_rate * (
        first_hat / (jnp.sqrt(second_hat) + epsilon) + decay_rate * param
    )
    return (param, first, second)


def value_kernel(where_ref, q_ref, k_ref, g_ref, o_ref):
    me = where_ref[0]
    rows = q_ref.shape[0]
    length = k_ref.shape[0]
    row = lax.broadcasted_iota(jnp.int32, (rows, length), 0)
    col = lax.broadcasted_iota(jnp.int32, (rows, length), 1)
    allowed = col <= jnp.where(col < rows, row, (me + 1) * rows - 1)
    keys = k_ref[...]
    total = jnp.zeros((length, HD), jnp.float32)
    for h in range(GRP):
        span = slice(h * HD, (h + 1) * HD)
        scores = lax.dot_general(
            q_ref[:, span], keys, (((1,), (1,)), ((), ())), preferred_element_type=jnp.float32
        ) * HD ** (-0.5)
        scores = jnp.where(allowed, scores, -jnp.inf)
        highest = jnp.max(scores, axis=-1, keepdims=True)
        weights = jnp.exp(scores - highest)
        probs = (weights / jnp.sum(weights, axis=-1, keepdims=True)).astype(jnp.bfloat16)
        total = total + lax.dot_general(
            probs, g_ref[:, span], (((0,), (0,)), ((), ())), preferred_element_type=jnp.float32
        )
    o_ref[...] = total


def value_terms(me, queries, keys_all, grad_out):
    rows = queries.shape[0]
    length = keys_all.shape[0]
    return pl.pallas_call(
        value_kernel,
        grid=(KV,),
        out_shape=jax.ShapeDtypeStruct((length, KV * HD), jnp.float32),
        in_specs=[
            pl.BlockSpec(memory_space=pltpu.SMEM),
            pl.BlockSpec((rows, GRP * HD), lambda g: (0, g)),
            pl.BlockSpec((length, HD), lambda g: (0, g)),
            pl.BlockSpec((rows, GRP * HD), lambda g: (0, g)),
        ],
        out_specs=pl.BlockSpec((length, HD), lambda g: (0, g)),
        cost_estimate=pl.CostEstimate(
            flops=4 * rows * length * HD * GRP * KV, bytes_accessed=4 << 20, transcendentals=0
        ),
    )(me[None], queries, keys_all, grad_out)


def pick_kernel(block_ref, x_ref, o_ref, p_ref):
    width = HD
    count = o_ref.shape[1] // width

    @pl.loop(0, count)
    def _(i):
        into = pl.ds(pl.multiple_of(i * width, width), width)
        o_ref[:, into] = x_ref[:, pl.ds(pl.multiple_of(block_ref[0, i] * width, width), width)]
        p_ref[:, into] = x_ref[:, pl.ds(pl.multiple_of(block_ref[1, i] * width, width), width)]


def pick(blocks, inputs):
    rows, wide = inputs.shape
    half = jax.ShapeDtypeStruct((rows, wide // 2), inputs.dtype)
    return pl.pallas_call(
        pick_kernel,
        out_shape=(half, half),
        in_specs=[
            pl.BlockSpec(memory_space=pltpu.SMEM),
            pl.BlockSpec(memory_space=pltpu.VMEM),
        ],
        out_specs=(pl.BlockSpec(memory_space=pltpu.VMEM),) * 2,
        cost_estimate=pl.CostEstimate(flops=0, bytes_accessed=4 << 20, transcendentals=0),
    )(blocks, inputs)


def swap(x, axis, size, bit):
    return lax.ppermute(x, axis, [(i, i ^ bit) for i in range(size)])


def halve(x, axis, bit_value):
    mine = lax.dynamic_index_in_dim(x, bit_value, axis, keepdims=False)
    other = lax.dynamic_index_in_dim(x, 1 - bit_value, axis, keepdims=False)
    return mine, other


def spread(onehot, state):
    return jnp.einsum(
        "ns,rsc->rnc",
        onehot.astype(state.dtype),
        state,
        precision=lax.Precision.HIGHEST if state.dtype == jnp.float32 else None,
        preferred_element_type=state.dtype,
    )


def moved_state(state, source_owner, source_rank, me, shards, sources, new_capacity):
    old_capacity = state.shape[1]
    rank_hot = source_rank[:, None] == jnp.arange(old_capacity)[None, :]
    mine = spread(rank_hot & (source_owner == me)[:, None], state)

    def my_part(x, first_shard, count):
        at = jnp.clip(me - first_shard, 0, count - 1) * new_capacity
        part = lax.dynamic_slice_in_dim(x, at, new_capacity, axis=1)
        inside = (me >= first_shard) & (me < first_shard + count)
        return jnp.where(inside, part, jnp.zeros_like(part))

    result = my_part(mine, 0, shards)

    def chain(route):
        out = jnp.zeros_like(result)
        come = None
        for step, (sender, receiver, low, high) in enumerate(route):
            count = high - low
            if step == 0 and old_capacity < count * new_capacity:
                raw = lax.ppermute(state, "shard", [(sender, receiver)])
                come = spread(
                    (rank_hot & (source_owner == sender)[:, None])[
                        low * new_capacity : high * new_capacity
                    ],
                    raw,
                )
            else:
                pay = mine[:, low * new_capacity : high * new_capacity]
                if come is not None:
                    skip = (low - before) * new_capacity
                    pay = pay + come[:, skip : skip + count * new_capacity]
                come = lax.ppermute(pay, "shard", [(sender, receiver)])
            before = low
            here = receiver - low
            part = come[:, here * new_capacity : (here + 1) * new_capacity]
            out = out + jnp.where(me == receiver, part, jnp.zeros_like(part))
        return out

    right = chain([(l, l + 1, l + 1, shards) for l in range(shards - 1)])
    left = chain([(l, l - 1, 0, l) for l in range(sources - 1, 0, -1)])
    return result + right + left


def local(queries, keys, grad_out, inputs, old_owner, new_owner, param_old, first_old, second_old):
    shards = lax.axis_size("shard")
    replicas = lax.axis_size("rep")
    me = lax.axis_index("shard")
    rep = lax.axis_index("rep")
    rows = queries.shape[0]
    blocks = old_owner.shape[0]
    block_rows = inputs.shape[1] // blocks
    own_rows = block_rows // replicas
    new_capacity = blocks // shards
    columns = KV * HD
    sources = shards - shards // 4
    bf16 = jnp.bfloat16

    chunks = [keys]
    for k in range(1, shards):
        chunks.append(lax.ppermute(keys, "shard", [(s, s + k) for s in range(shards - k)]))

    new_slot = new_owner * new_capacity + owner_ranks(new_owner, shards)
    match = new_slot[None, :] == jnp.arange(blocks, dtype=jnp.int32)[:, None]

    def by_slot(table):
        return jnp.sum(jnp.where(match, table[None, :], 0), axis=1)

    new_block = by_slot(jnp.arange(blocks, dtype=jnp.int32))
    source_owner = by_slot(old_owner)
    source_rank = by_slot(owner_ranks(old_owner, shards))

    parity = me % 2
    halves = new_block.reshape(shards // 2, 2, new_capacity).transpose(1, 0, 2).reshape(2, -1)
    mine_first = jnp.where(parity == 0, halves, halves[::-1])
    kept, sent = pick(mine_first, inputs)
    arrived = swap(sent, "shard", shards, 1)

    moved = [
        moved_state(x, source_owner, source_rank, me, shards, sources, new_capacity)
        for x in (first_old.astype(bf16), second_old.astype(bf16), param_old)
    ]
    first, second, param = (x.astype(jnp.float32) for x in moved)

    part = value_terms(me, queries, jnp.concatenate(chunks, axis=0), grad_out)
    values = part[:rows]
    for k in range(1, shards):
        values = values + lax.ppermute(
            part[k * rows : (k + 1) * rows], "shard", [(s, s - k) for s in range(k, shards)]
        )
    values = values.astype(bf16)
    values_pair = swap(values, "shard", shards, 1)

    contract = (((0,), (0,)), ((), ()))
    product = lax.dot_general(
        jnp.concatenate([kept, arrived], axis=0),
        jnp.concatenate([values, values_pair], axis=0),
        contract,
        preferred_element_type=jnp.float32,
    )
    bits = [1 << n for n in range(replicas.bit_length() - 1)]
    split = tuple(2 for _ in bits)
    product = product.reshape((-1,) + split + (own_rows, columns))

    def scatter(x, order):
        left = sorted(order, reverse=True)
        for bit in order:
            mine, other = halve(x, 1 + left.index(bit), (rep // bit) % 2)
            x = mine + swap(other.astype(bf16), "rep", replicas, bit).astype(jnp.float32)
            left.remove(bit)
        return x

    mine, other = halve(product, len(bits), rep % 2)
    product = mine + swap(other.astype(bf16), "rep", replicas, 1).astype(jnp.float32)
    product = product.reshape((2, -1) + product.shape[1:])
    a = scatter(product[0], bits[1:])
    b = scatter(product[1], bits[:0:-1])
    gradient = jnp.concatenate([a, b], axis=0).reshape(
        shards // 2, new_capacity, own_rows, columns
    )
    pair = me // 2
    total = lax.dynamic_index_in_dim(gradient, pair, 0, keepdims=False)
    for k in range(1, shards // 2):
        out = lax.dynamic_index_in_dim(gradient, (pair + k) % (shards // 2), 0, keepdims=False)
        total = total + lax.ppermute(
            out.astype(bf16), "shard", [(s, (s + 2 * k) % shards) for s in range(shards)]
        ).astype(jnp.float32)
    gradient = total.transpose(1, 0, 2)

    param_new, first_new, second_new = adamw(param, first, second, gradient)
    working = param_new.astype(bf16)
    every = [working]
    for k in range(1, shards):
        every.append(
            lax.ppermute(working, "shard", [(s, (s + k) % shards) for s in range(shards)])
        )
    stacked = jnp.concatenate(every, axis=1)
    at = ((me - new_slot // new_capacity) % shards) * new_capacity + new_slot % new_capacity
    weights = spread(at[:, None] == jnp.arange(blocks)[None, :], stacked)
    return (param_new, first_new, second_new, weights)


def tables(old_ref, new_ref, tab_ref, old_capacity, capacity):
    count = old_ref.shape[1]
    sub = lax.broadcasted_iota(jnp.int32, (count, count), 0)
    lane = lax.broadcasted_iota(jnp.int32, (count, count), 1)

    def ranks(ref):
        across = jnp.broadcast_to(ref[...], (count, count))
        down = jnp.sum(jnp.where(sub == lane, across, 0), axis=1, keepdims=True)
        same = across == down
        below = jnp.sum(jnp.where(same & (lane < sub), 1, 0), axis=1, keepdims=True)
        return down, below

    old, old_rank = ranks(old_ref)
    new, new_rank = ranks(new_ref)
    hit = new * capacity + new_rank == lane
    old_rank = jnp.minimum(old_rank, old_capacity - 1)
    for at, table in enumerate((sub, old, old_rank)):
        tab_ref[at : at + 1, :count] = jnp.sum(jnp.where(hit, table, 0), axis=0, keepdims=True)


def fused_kernel(
    old_ref, new_ref, q_h, key_h, g_h, x_h, p_h, f_h, s_h,
    pn_h, fn_h, sn_h, wall_h,
    tab, tab_v, q_ref, g_ref, x_ref, state, kbuf, part, vo, v_in, vals, xs, xt, xo,
    st_own, raw_a0, raw_a1, raw_a2, raw_a3, raw_b0, raw_b1, raw_b2, raw_b3,
    r_out, a_in, l_out, l_in, d_out, d_in, settled,
    gbuf, pass_out, pass_in, mid_out, mid_in, fin_out, fin_in, grad, tmp, wall,
    load_sem, k_sem, x_sem, xl_sem, v_sem, va_sem, raw_sem, st_sem,
    pass_sem, mid_sem, fin_sem, w_sem, wo_sem,
):
    bf16, f32 = jnp.bfloat16, jnp.float32
    me, rep = lax.axis_index("shard"), lax.axis_index("rep")
    shards = kbuf.shape[1]
    rows = key_h.shape[0]
    length = shards * rows
    cap = pn_h.shape[1]
    blocks = xs.shape[1]
    own_rows = xs.shape[2]
    replicas = xs.shape[0]
    slots = cap * own_rows
    pieces = x_sem.shape[0]
    sources = shards - 1
    raw_a = (raw_a0, raw_a1, raw_a2, raw_a3)
    raw_b = (raw_b0, raw_b1, raw_b2, raw_b3)
    bits = (rep % 2, (rep // 2) % 2, rep // 4)
    has_left, has_right = me > 0, me < shards - 1
    edge = (me == 0) | (me == shards - 1)
    inner = (me > 0) & (me < shards - 1)
    pair = me + 1 - 2 * (me % 2)
    mid = shards - 1 - me
    side = me // 2
    near = 2 - side
    far = 3 - 3 * side
    left, right = (rep, me - 1), (rep, me + 1)

    def peer(k):
        return sum(
            (1 << n) * (bit + ((k >> n) & 1) * (1 - 2 * bit)) for n, bit in enumerate(bits)
        )

    def send(src, dst, sem, target):
        return pltpu.make_async_remote_copy(
            src_ref=src, dst_ref=dst, send_sem=sem.at[0], recv_sem=sem.at[1],
            device_id=target, device_id_type=pl.DeviceIdType.MESH,
        )

    def cols(g):
        return pl.ds(g * HD, HD)

    def key_load(g):
        return pltpu.make_async_copy(key_h.at[:, cols(g)], kbuf.at[g, 0], load_sem.at[g])

    wide = x_h.shape[1] // pieces

    def x_load(p):
        span = pl.ds(p * wide, wide)
        return pltpu.make_async_copy(x_h.at[:, span], x_ref.at[:, span], load_sem.at[KV + p])

    late = KV + pieces
    q_load = pltpu.make_async_copy(q_h, q_ref, load_sem.at[late])
    g_load = pltpu.make_async_copy(g_h, g_ref, load_sem.at[late + 1])
    s_loads = [
        pltpu.make_async_copy(src, state.at[i], load_sem.at[late + 2 + i])
        for i, src in enumerate((p_h, f_h, s_h))
    ]
    for g in range(KV):
        key_load(g).start()
    for copy in s_loads:
        copy.start()
    for p in range(pieces):
        x_load(p).start()
    q_load.start()
    g_load.start()

    barrier = pltpu.get_barrier_semaphore()

    def greet(target):
        pl.semaphore_signal(barrier, inc=1, device_id=target, device_id_type=pl.DeviceIdType.MESH)

    for k in range(1, replicas):
        greet((peer(k), me))
    pl.when(has_left)(lambda: greet(left))
    pl.when(has_right)(lambda: greet(right))
    tables(old_ref, new_ref, tab_v, st_own.shape[1], cap)
    tab_load = pltpu.make_async_copy(tab_v, tab, load_sem.at[late + 5])
    tab_load.start()
    for g in range(KV):
        key_load(g).wait()
    tab_load.wait()
    pl.semaphore_wait(barrier, replicas + jnp.where(inner, 1, 0))

    def key_copy(g, j):
        return send(kbuf.at[g, j], kbuf.at[g, j + 1], k_sem.at[g, j], right)

    for g in range(KV):
        pl.when(has_right)(lambda g=g: key_copy(g, 0).start())

    def key_relay(j):
        for g in range(KV):
            @pl.when((me >= j) & has_right)
            def _(g=g):
                key_copy(g, j - 1).wait_recv()
                if j < shards - 1:
                    key_copy(g, j).start()

            @pl.when(me < j)
            def _(g=g):
                kbuf[g, j] = jnp.zeros(kbuf.shape[2:], kbuf.dtype)

    for copy in s_loads:
        copy.wait()

    @pl.loop(0, st_own.shape[1])
    def _(s):
        for g in range(KV):
            for i in range(3):
                st_own[g, s, i] = state[i, s, :, g * HD : (g + 1) * HD].astype(bf16)

    def raw_right(g):
        return send(st_own.at[g], raw_a[g], raw_sem.at[g, 0], right)

    def raw_left(g):
        return send(st_own.at[g], raw_b[g], raw_sem.at[g, 1], left)

    def send_left(g):
        pl.when(me == sources - 1)(lambda: raw_left(g).start())

    for g in range(KV):
        pl.when(me == 0)(lambda g=g: raw_right(g).start())
    for g in range(3):
        send_left(g)

    group = blocks // pieces

    def x_copy(p, k):
        span = pl.ds(p * group, group)
        return send(
            xs.at[peer(k), span],
            xt.at[span, :, pl.ds(pl.multiple_of(rep * rows, rows), rows)],
            x_sem.at[p, k],
            (peer(k), me),
        )

    def x_keep(p):
        span = pl.ds(p * group, group)
        return pltpu.make_async_copy(
            xs.at[rep, span],
            xt.at[span, :, pl.ds(pl.multiple_of(rep * rows, rows), rows)],
            xl_sem.at[p],
        )

    for p in range(pieces):
        x_load(p).wait()

        @pl.loop(p * group, (p + 1) * group, unroll=4)
        def _(b):
            block = x_ref[:, pl.ds(pl.multiple_of(b * HD, HD), HD)].T
            xs[:, b] = block.reshape(replicas, own_rows, rows)

        for k in (2, 4, 6, 3, 5, 7, 1):
            x_copy(p, k).start()
        x_keep(p).start()
        if p > 1:
            key_relay(p - 1)

    for j in range(pieces - 1, shards):
        key_relay(j)

    def v_copy(g, c):
        return send(vo.at[g, c], v_in.at[g, c], v_sem.at[g, c], left)

    def va_copy(g, k):
        return send(vals.at[g, rep], vals.at[g, rep], va_sem.at[g, k], (peer(k), me))

    def va_relay(g, k):
        return send(vals.at[g, peer(k)], vals.at[g, peer(k)], va_sem.at[g, k + 1], (peer(1), me))

    def finish(g, value):
        vals[g, rep] = value.astype(bf16)
        for k in (6, 2, 4, 1):
            va_copy(g, k).start()

    q_load.wait()
    g_load.wait()
    row = lax.broadcasted_iota(jnp.int32, (rows, length), 0)
    col = lax.broadcasted_iota(jnp.int32, (rows, length), 1)
    allowed = col <= jnp.where(col < rows, row, (me + 1) * rows - 1)

    @pl.loop(0, KV)
    def _(g):
        @pl.when(me == shards - 1)
        def _():
            for j in range(shards - 1):
                key_copy(g, j).wait_recv()

        keys = kbuf[g].reshape(length, HD)
        total = jnp.zeros((length, HD), f32)
        for h in range(GRP):
            span = pl.ds(pl.multiple_of(g * (GRP * HD) + h * HD, HD), HD)
            scores = lax.dot_general(
                q_ref[:, span], keys, (((1,), (1,)), ((), ())), preferred_element_type=f32
            ) * HD ** (-0.5)
            scores = jnp.where(allowed, scores, -jnp.inf)
            highest = jnp.max(scores, axis=-1, keepdims=True)
            weights = jnp.exp(scores - highest)
            probs = (weights / jnp.sum(weights, axis=-1, keepdims=True)).astype(bf16)
            total = total + lax.dot_general(
                probs, g_ref[:, span], (((0,), (0,)), ((), ())), preferred_element_type=f32
            )
        part[g] = total.reshape(shards, rows, HD)

        @pl.when(me == shards - 1)
        def _():
            for c in range(shards - 1):
                vo[g, c] = part[g, shards - 1 - c]
                v_copy(g, c).start()
            finish(g, part[g, 0])

    def chain(g, role):
        @pl.when(me == role)
        def _():
            for c in range(role):
                v_copy(g, c).wait_recv()
                vo[g, c] = part[g, role - c] + v_in[g, c]
                v_copy(g, c).start()
            v_copy(g, role).wait_recv()
            finish(g, part[g, 0] + v_in[g, role])

    def r_copy(g, i):
        return send(r_out.at[g, i], a_in.at[g, i], st_sem.at[g, i], right)

    def l_copy(g):
        return send(l_out.at[g], l_in.at[g], st_sem.at[g, 2], left)

    def d_copy(g):
        return send(d_out.at[g], d_in.at[g], st_sem.at[g, 3], right)

    def choose(g, owner, first, out, other):
        @pl.loop(0, cap)
        def _(j):
            s = first * cap + j
            at = tab[2, s]
            out[j] = jnp.where(tab[1, s] == owner, st_own[g, at], other(j, at))

    def route_right(g):
        @pl.when(me == 1)
        def _():
            raw_right(g).wait_recv()
            for i, first in enumerate((3, 2)):
                choose(g, 1, first, r_out.at[g, i], lambda j, at: raw_a[g][at])
                r_copy(g, i).start()

    def route_left(g):
        @pl.when(me == 1)
        def _():
            raw_left(g).wait_recv()
            choose(g, 1, 0, l_out.at[g], lambda j, at: raw_b[g][at])
            l_copy(g).start()

    def route_last(g):
        @pl.when(me == 2)
        def _():
            r_copy(g, 0).wait_recv()
            choose(g, 2, 3, d_out.at[g], lambda j, at: a_in[g, 0, j])
            d_copy(g).start()

    def settle(g):
        def take(other):
            @pl.loop(0, cap)
            def _(j):
                s = me * cap + j
                at = tab[2, s]
                mine = tab[1, s] == me
                moved = other(j, s, at)
                for i in range(3):
                    settled[i, j] = jnp.where(
                        mine, state[i, at, :, g * HD : (g + 1) * HD], moved[i].astype(f32)
                    )

        @pl.when(me == 0)
        def _():
            l_copy(g).wait_recv()
            take(lambda j, s, at: l_in[g, j])

        @pl.when(me == 1)
        def _():
            take(lambda j, s, at: jnp.where(tab[1, s] == 0, raw_a[g][at], raw_b[g][at]))

        @pl.when(me == 2)
        def _():
            r_copy(g, 1).wait_recv()
            take(lambda j, s, at: a_in[g, 1, j])

        @pl.when(me == 3)
        def _():
            d_copy(g).wait_recv()
            take(lambda j, s, at: d_in[g, j])

    def pass_copy(g, i):
        return send(pass_out.at[g, i], pass_in.at[g, i], pass_sem.at[g, i], (rep, pair))

    def mid_copy(g, i):
        return send(mid_out.at[g, i], mid_in.at[g, i], mid_sem.at[g, i], (rep, mid))

    def fin_copy(g):
        return send(fin_out.at[g], fin_in.at[g], fin_sem.at[g], (rep, pair))

    def arrange():
        for p in range(pieces):
            for k in range(1, replicas):
                x_copy(p, k).wait_recv()
            x_keep(p).wait()

        @pl.loop(0, blocks)
        def _(s):
            xo[s] = xt[tab[0, s]]

    def relay(g):
        for k in (2, 4, 6):
            va_copy(g, k).wait_recv()
            va_relay(g, k).start()

    def product(g):
        va_copy(g, 1).wait_recv()
        for k in (2, 4, 6):
            va_relay(g, k).wait_recv()
        value = vals[g].reshape(replicas * rows, HD)

        @pl.loop(0, shards)
        def _(o):
            block = xo[pl.ds(o * cap, cap)].reshape(slots, replicas * rows)
            gbuf[g, o] = jnp.dot(block, value, preferred_element_type=f32)

        @pl.when(edge)
        def _():
            for i, to in enumerate((far, near)):
                pass_out[g, i] = gbuf[g, to].astype(bf16)
                pass_copy(g, i).start()

    def final(g, role):
        @pl.when(me == role)
        def _():
            fin_out[g] = gbuf[g, pair]
            fin_copy(g).start()

    def cross(g, role):
        @pl.when(me == role)
        def _():
            for i, to in enumerate((far, near)):
                pass_copy(g, i).wait_recv()
                mid_out[g, i] = (gbuf[g, to] + pass_in[g, i].astype(f32)).astype(bf16)
                mid_copy(g, i).start()

    def back(g, role):
        @pl.when(me == role)
        def _():
            mid_copy(g, 0).wait_recv()
            fin_out[g] = gbuf[g, pair] + mid_in[g, 0].astype(f32)
            fin_copy(g).start()

    def w_copy(g, t, direction):
        origin = (me - t, me + t)[direction]
        ref = wall.at[g, origin]
        return send(ref, ref, w_sem.at[g, t, direction], (right, left)[direction])

    def w_out(g, origin):
        at = pl.ds(pl.multiple_of(origin * cap, cap), cap)
        return pltpu.make_async_copy(wall.at[g, origin], wall_h.at[:, at, cols(g)], wo_sem.at[g, origin])

    def update(g):
        settle(g)
        fin_copy(g).wait_recv()

        @pl.when(edge)
        def _():
            grad[...] = gbuf[g, me] + fin_in[g]

        @pl.when(inner)
        def _():
            mid_copy(g, 1).wait_recv()
            grad[...] = gbuf[g, me] + fin_in[g] + mid_in[g, 1].astype(f32)

        @pl.loop(0, cap)
        def _(j):
            at = pl.ds(pl.multiple_of(j * own_rows, own_rows), own_rows)
            new = adamw(settled[0, j], settled[1, j], settled[2, j], grad[at, :])
            for i in range(3):
                tmp[i, at, :] = new[i]

        for r in range(own_rows):
            param = tmp[0, pl.ds(r, cap, stride=own_rows), :]
            pn_h[r, :, g * HD : (g + 1) * HD] = param
            wall[g, me, r] = param.astype(bf16)
        pl.when(has_right)(lambda: w_copy(g, 0, 0).start())
        pl.when(has_left)(lambda: w_copy(g, 0, 1).start())
        for r in range(own_rows):
            for i in (1, 2):
                out = (fn_h, sn_h)[i - 1]
                out[r, :, g * HD : (g + 1) * HD] = tmp[i, pl.ds(r, cap, stride=own_rows), :]
        w_out(g, me).start()

    def gather_right(g, t):
        @pl.when(me >= t)
        def _():
            arrived = wall.at[g, me - t]
            send(arrived, arrived, w_sem.at[g, t - 1, 0], right).wait_recv()
            if t < shards - 1:
                pl.when(has_right)(lambda: w_copy(g, t, 0).start())
            w_out(g, me - t).start()

    def gather_left(g, t):
        @pl.when(me + t < shards)
        def _():
            arrived = wall.at[g, me + t]
            send(arrived, arrived, w_sem.at[g, t - 1, 1], left).wait_recv()
            if t < shards - 1:
                pl.when(has_left)(lambda: w_copy(g, t, 1).start())
            w_out(g, me + t).start()

    steps = [
        (route_right, 0), (chain, 0, 2), (route_last, 0), (route_left, 0), (chain, 0, 0), (route_right, 1),
        (chain, 0, 1), (chain, 1, 1), (chain, 1, 2), (route_left, 1), (chain, 2, 2), (chain, 3, 2),
        (send_left, 3), (chain, 1, 0), (relay, 0), (arrange,), (product, 0), (cross, 0, 2),
        (route_last, 1), (chain, 2, 1), (route_right, 2), (final, 0, 0), (chain, 2, 0), (relay, 1),
        (product, 1), (cross, 0, 1), (chain, 3, 1), (relay, 2), (product, 2), (route_last, 2),
        (route_left, 2), (chain, 3, 0), (back, 0, 1), (cross, 1, 1), (cross, 1, 2), (final, 1, 0),
        (relay, 3), (product, 3), (cross, 3, 2), (final, 3, 0), (final, 0, 3), (back, 0, 2),
        (route_right, 3), (final, 2, 3), (final, 1, 3), (update, 0), (route_left, 3), (final, 3, 3),
        (back, 3, 1), (back, 1, 2), (cross, 2, 1), (back, 1, 1), (cross, 2, 2), (back, 2, 1),
        (final, 2, 0), (update, 1), (cross, 3, 1), (route_last, 3), (gather_left, 0, 1), (gather_right, 0, 1),
        (back, 2, 2), (update, 2), (gather_left, 1, 1), (back, 3, 2), (update, 3), (gather_right, 2, 1),
        (gather_left, 0, 2), (gather_left, 0, 3), (gather_right, 1, 3), (gather_left, 3, 3), (gather_right, 3, 3), (gather_left, 2, 1),
        (gather_right, 3, 1), (gather_right, 1, 1), (gather_left, 2, 2), (gather_left, 3, 1), (gather_right, 2, 2), (gather_right, 1, 2),
        (gather_right, 3, 2), (gather_left, 2, 3), (gather_right, 0, 3), (gather_right, 0, 2), (gather_left, 1, 2), (gather_left, 3, 2),
        (gather_left, 1, 3), (gather_right, 2, 3),
    ]
    for step, *at in steps:
        step(*at)

    for g in range(KV):
        for j in range(shards - 1):
            pl.when(has_right & (me >= j))(lambda g=g, j=j: key_copy(g, j).wait_send())
        for c in range(shards - 1):
            pl.when(me > c)(lambda g=g, c=c: v_copy(g, c).wait_send())
        for k in (6, 2, 4, 1):
            va_copy(g, k).wait_send()
        for k in (2, 4, 6):
            va_relay(g, k).wait_send()

        @pl.when(me == 0)
        def _(g=g):
            raw_right(g).wait_send()

        @pl.when(me == 1)
        def _(g=g):
            r_copy(g, 0).wait_send()
            r_copy(g, 1).wait_send()
            l_copy(g).wait_send()

        @pl.when(me == 2)
        def _(g=g):
            raw_left(g).wait_send()
            d_copy(g).wait_send()

        @pl.when(edge)
        def _(g=g):
            for i in range(2):
                pass_copy(g, i).wait_send()

        @pl.when(inner)
        def _(g=g):
            for i in range(2):
                mid_copy(g, i).wait_send()

        fin_copy(g).wait_send()
        for t in range(shards - 1):
            pl.when(has_right & (me >= t))(lambda g=g, t=t: w_copy(g, t, 0).wait_send())
            pl.when(has_left & (me + t < shards))(lambda g=g, t=t: w_copy(g, t, 1).wait_send())
        for o in range(shards):
            w_out(g, o).wait()
    for p in range(pieces):
        for k in range(1, replicas):
            x_copy(p, k).wait_send()


def finish_kernel(new_ref, pn_ref, fn_ref, sn_ref, wall_ref, pn_h, fn_h, sn_h, w_h, w_ref, sem):
    rows, blocks = w_ref.shape[:2]
    cap = pn_ref.shape[1]
    step = 4
    copies = [
        pltpu.make_async_copy(src, dst, sem.at[i])
        for i, (src, dst) in enumerate(((pn_ref, pn_h), (fn_ref, fn_h), (sn_ref, sn_h)))
    ]
    for copy in copies:
        copy.start()
    sub = lax.broadcasted_iota(jnp.int32, (blocks, blocks), 0)
    lane = lax.broadcasted_iota(jnp.int32, (blocks, blocks), 1)
    across = jnp.broadcast_to(new_ref[...], (blocks, blocks))
    owner = jnp.sum(jnp.where(sub == lane, across, 0), axis=1, keepdims=True)
    rank = jnp.sum(jnp.where((across == owner) & (lane < sub), 1, 0), axis=1, keepdims=True)
    hot = jnp.where(owner * cap + rank == lane, 1.0, 0.0).astype(w_ref.dtype)
    for n in range(rows // step):
        for r in range(n * step, (n + 1) * step):
            w_ref[r] = jnp.dot(hot, wall_ref[r], preferred_element_type=jnp.float32).astype(w_ref.dtype)
        span = pl.ds(n * step, step)
        copies.append(pltpu.make_async_copy(w_ref.at[span], w_h.at[span], sem.at[3 + n]))
        copies[-1].start()
    for copy in copies:
        copy.wait()


def fused(queries, keys, grad_out, inputs, old_owner, new_owner, param_old, first_old, second_old):
    shards = lax.axis_size("shard")
    replicas = lax.axis_size("rep")
    rows = queries.shape[0]
    blocks = old_owner.shape[0]
    own_rows = inputs.shape[1] // blocks // replicas
    cap = blocks // shards
    width = KV * HD
    old_cap = param_old.shape[1]
    bf16, f32 = jnp.bfloat16, jnp.float32
    pieces = 4

    V = pltpu.VMEM
    slot = V((own_rows, cap, width), f32)
    tokens = replicas * rows
    slots = cap * own_rows

    def state(*count):
        return V((*count, 3, own_rows, HD), bf16)

    def dma(*shape):
        return pltpu.SemaphoreType.DMA(shape)

    outs = pl.pallas_call(
        fused_kernel,
        out_shape=(slot, slot, slot, V((own_rows, blocks, width), bf16)),
        in_specs=[pl.BlockSpec(memory_space=pltpu.VMEM)] * 2 + [pl.BlockSpec(memory_space=pl.ANY)] * 7,
        out_specs=(pl.BlockSpec(memory_space=pltpu.VMEM),) * 4,
        scratch_shapes=[
            pltpu.SMEM((8, 128), jnp.int32), V((8, 128), jnp.int32),
            V(queries.shape, bf16), V(grad_out.shape, bf16), V(inputs.shape, bf16),
            V((3, old_cap, own_rows, width), f32),
            V((KV, shards, rows, HD), bf16),
            V((KV, shards, rows, HD), f32),
            V((KV, shards - 1, rows, HD), f32), V((KV, shards - 1, rows, HD), f32),
            V((KV, replicas, rows, HD), bf16),
            V((replicas, blocks, own_rows, rows), bf16),
            V((blocks, own_rows, tokens), bf16), V((blocks, own_rows, tokens), bf16),
            state(KV, old_cap),
            *[state(old_cap)] * 8,
            state(KV, 2, cap), state(KV, 2, cap),
            state(KV, cap), state(KV, cap), state(KV, cap), state(KV, cap),
            V((3, cap, own_rows, HD), f32),
            V((KV, shards, slots, HD), f32),
            *[V((KV, 2, slots, HD), bf16)] * 4,
            V((KV, slots, HD), f32), V((KV, slots, HD), f32),
            V((slots, HD), f32), V((3, slots, HD), f32),
            V((KV, shards, own_rows, cap, HD), bf16),
            dma(KV + pieces + 6), dma(KV, shards - 1, 2), dma(pieces, replicas, 2), dma(pieces),
            dma(KV, shards - 1, 2), dma(KV, replicas, 2), dma(KV, 2, 2), dma(KV, 4, 2),
            dma(KV, 2, 2), dma(KV, 2, 2), dma(KV, 2), dma(KV, shards - 1, 2, 2),
            dma(KV, shards),
        ],
        compiler_params=pltpu.CompilerParams(
            collective_id=0, has_side_effects=True, vmem_limit_bytes=61 << 20
        ),
    )(
        old_owner[None], new_owner[None], queries, keys, grad_out, inputs,
        *[jnp.transpose(x, (1, 0, 2)) for x in (param_old, first_old, second_old)],
    )
    return pl.pallas_call(
        finish_kernel,
        out_shape=tuple(
            jax.ShapeDtypeStruct((own_rows, count, width), kind)
            for count, kind in ((cap, f32), (cap, f32), (cap, f32), (blocks, bf16))
        ),
        in_specs=[pl.BlockSpec(memory_space=pltpu.VMEM)] * 5,
        out_specs=(pl.BlockSpec(memory_space=pl.ANY),) * 4,
        scratch_shapes=[V((own_rows, blocks, width), bf16), dma(own_rows // 4 + 3)],
        compiler_params=pltpu.CompilerParams(vmem_limit_bytes=8 << 20),
    )(new_owner[None], *[pltpu.with_memory_space_constraint(x, pltpu.VMEM) for x in outs])


def solution(mesh):
    placed = (
        P(("rep", "shard"), None),
        P(("rep", "shard"), None),
        P(("rep", "shard"), None),
        P(("rep", "shard"), None),
        P(),
        P(),
        P("rep", "shard", None),
        P("rep", "shard", None),
        P("rep", "shard", None),
    )
    small = mesh.shape["shard"] == 4 and mesh.shape["rep"] == 8
    return jax.shard_map(
        fused if small else local,
        mesh=mesh,
        in_specs=placed,
        out_specs=(
            P("rep", "shard", None),
            P("rep", "shard", None),
            P("rep", "shard", None),
            P("rep", None, None),
        ),
        check_vma=False,
    )
```

```python
import functools

import jax
import jax.numpy as jnp
from jax import lax
from jax.experimental import pallas as pl
from jax.experimental.pallas import tpu as pltpu
from jax.sharding import PartitionSpec as P

KV = 4
HD = 128
GRP = 8
STEP = 1000

beta_first = 0.9
beta_second = 0.95
learning_rate = 0.02
decay_rate = 0.1
epsilon = 1e-08


def owner_ranks(owner, owners):
    onehot = (owner[:, None] == jnp.arange(owners, dtype=jnp.int32)[None, :]).astype(jnp.int32)
    running = jnp.cumsum(onehot, axis=0)
    return jnp.sum(running * onehot, axis=1) - 1


def adamw(param, first, second, gradient):
    first = beta_first * first + (1.0 - beta_first) * gradient
    second = beta_second * second + (1.0 - beta_second) * gradient * gradient
    first_hat = first / (1.0 - beta_first**STEP)
    second_hat = second / (1.0 - beta_second**STEP)
    param = param - learning_rate * (
        first_hat / (jnp.sqrt(second_hat) + epsilon) + decay_rate * param
    )
    return (param, first, second)


def value_kernel(where_ref, q_ref, k_ref, g_ref, o_ref):
    me = where_ref[0]
    rows = q_ref.shape[0]
    length = k_ref.shape[0]
    row = lax.broadcasted_iota(jnp.int32, (rows, length), 0)
    col = lax.broadcasted_iota(jnp.int32, (rows, length), 1)
    allowed = col <= jnp.where(col < rows, row, (me + 1) * rows - 1)
    keys = k_ref[...]
    total = jnp.zeros((length, HD), jnp.float32)
    for h in range(GRP):
        span = slice(h * HD, (h + 1) * HD)
        scores = lax.dot_general(
            q_ref[:, span], keys, (((1,), (1,)), ((), ())), preferred_element_type=jnp.float32
        ) * HD ** (-0.5)
        scores = jnp.where(allowed, scores, -jnp.inf)
        highest = jnp.max(scores, axis=-1, keepdims=True)
        weights = jnp.exp(scores - highest)
        probs = (weights / jnp.sum(weights, axis=-1, keepdims=True)).astype(jnp.bfloat16)
        total = total + lax.dot_general(
            probs, g_ref[:, span], (((0,), (0,)), ((), ())), preferred_element_type=jnp.float32
        )
    o_ref[...] = total


def value_terms(me, queries, keys_all, grad_out):
    rows = queries.shape[0]
    length = keys_all.shape[0]
    return pl.pallas_call(
        value_kernel,
        grid=(KV,),
        out_shape=jax.ShapeDtypeStruct((length, KV * HD), jnp.float32),
        in_specs=[
            pl.BlockSpec(memory_space=pltpu.SMEM),
            pl.BlockSpec((rows, GRP * HD), lambda g: (0, g)),
            pl.BlockSpec((length, HD), lambda g: (0, g)),
            pl.BlockSpec((rows, GRP * HD), lambda g: (0, g)),
        ],
        out_specs=pl.BlockSpec((length, HD), lambda g: (0, g)),
        cost_estimate=pl.CostEstimate(
            flops=4 * rows * length * HD * GRP * KV, bytes_accessed=4 << 20, transcendentals=0
        ),
    )(me[None], queries, keys_all, grad_out)


def pick_kernel(block_ref, x_ref, o_ref, p_ref):
    width = HD
    count = o_ref.shape[1] // width

    @pl.loop(0, count)
    def _(i):
        into = pl.ds(pl.multiple_of(i * width, width), width)
        o_ref[:, into] = x_ref[:, pl.ds(pl.multiple_of(block_ref[0, i] * width, width), width)]
        p_ref[:, into] = x_ref[:, pl.ds(pl.multiple_of(block_ref[1, i] * width, width), width)]


def pick(blocks, inputs):
    rows, wide = inputs.shape
    half = jax.ShapeDtypeStruct((rows, wide // 2), inputs.dtype)
    return pl.pallas_call(
        pick_kernel,
        out_shape=(half, half),
        in_specs=[
            pl.BlockSpec(memory_space=pltpu.SMEM),
            pl.BlockSpec(memory_space=pltpu.VMEM),
        ],
        out_specs=(pl.BlockSpec(memory_space=pltpu.VMEM),) * 2,
        cost_estimate=pl.CostEstimate(flops=0, bytes_accessed=4 << 20, transcendentals=0),
    )(blocks, inputs)


def swap(x, axis, size, bit):
    return lax.ppermute(x, axis, [(i, i ^ bit) for i in range(size)])


def halve(x, axis, bit_value):
    mine = lax.dynamic_index_in_dim(x, bit_value, axis, keepdims=False)
    other = lax.dynamic_index_in_dim(x, 1 - bit_value, axis, keepdims=False)
    return mine, other


def spread(onehot, state):
    return jnp.einsum(
        "ns,rsc->rnc",
        onehot.astype(state.dtype),
        state,
        precision=lax.Precision.HIGHEST if state.dtype == jnp.float32 else None,
        preferred_element_type=state.dtype,
    )


def moved_state(state, source_owner, source_rank, me, shards, sources, new_capacity):
    old_capacity = state.shape[1]
    rank_hot = source_rank[:, None] == jnp.arange(old_capacity)[None, :]
    mine = spread(rank_hot & (source_owner == me)[:, None], state)

    def my_part(x, first_shard, count):
        at = jnp.clip(me - first_shard, 0, count - 1) * new_capacity
        part = lax.dynamic_slice_in_dim(x, at, new_capacity, axis=1)
        inside = (me >= first_shard) & (me < first_shard + count)
        return jnp.where(inside, part, jnp.zeros_like(part))

    result = my_part(mine, 0, shards)

    def chain(route):
        out = jnp.zeros_like(result)
        come = None
        for step, (sender, receiver, low, high) in enumerate(route):
            count = high - low
            if step == 0 and old_capacity < count * new_capacity:
                raw = lax.ppermute(state, "shard", [(sender, receiver)])
                come = spread(
                    (rank_hot & (source_owner == sender)[:, None])[
                        low * new_capacity : high * new_capacity
                    ],
                    raw,
                )
            else:
                pay = mine[:, low * new_capacity : high * new_capacity]
                if come is not None:
                    skip = (low - before) * new_capacity
                    pay = pay + come[:, skip : skip + count * new_capacity]
                come = lax.ppermute(pay, "shard", [(sender, receiver)])
            before = low
            here = receiver - low
            part = come[:, here * new_capacity : (here + 1) * new_capacity]
            out = out + jnp.where(me == receiver, part, jnp.zeros_like(part))
        return out

    right = chain([(l, l + 1, l + 1, shards) for l in range(shards - 1)])
    left = chain([(l, l - 1, 0, l) for l in range(sources - 1, 0, -1)])
    return result + right + left


def local(queries, keys, grad_out, inputs, old_owner, new_owner, param_old, first_old, second_old):
    shards = lax.axis_size("shard")
    replicas = lax.axis_size("rep")
    me = lax.axis_index("shard")
    rep = lax.axis_index("rep")
    rows = queries.shape[0]
    blocks = old_owner.shape[0]
    block_rows = inputs.shape[1] // blocks
    own_rows = block_rows // replicas
    new_capacity = blocks // shards
    columns = KV * HD
    sources = shards - shards // 4
    bf16 = jnp.bfloat16

    chunks = [keys]
    for k in range(1, shards):
        chunks.append(lax.ppermute(keys, "shard", [(s, s + k) for s in range(shards - k)]))

    new_slot = new_owner * new_capacity + owner_ranks(new_owner, shards)
    match = new_slot[None, :] == jnp.arange(blocks, dtype=jnp.int32)[:, None]

    def by_slot(table):
        return jnp.sum(jnp.where(match, table[None, :], 0), axis=1)

    new_block = by_slot(jnp.arange(blocks, dtype=jnp.int32))
    source_owner = by_slot(old_owner)
    source_rank = by_slot(owner_ranks(old_owner, shards))

    parity = me % 2
    halves = new_block.reshape(shards // 2, 2, new_capacity).transpose(1, 0, 2).reshape(2, -1)
    mine_first = jnp.where(parity == 0, halves, halves[::-1])
    kept, sent = pick(mine_first, inputs)
    arrived = swap(sent, "shard", shards, 1)

    moved = [
        moved_state(x, source_owner, source_rank, me, shards, sources, new_capacity)
        for x in (first_old.astype(bf16), second_old.astype(bf16), param_old)
    ]
    first, second, param = (x.astype(jnp.float32) for x in moved)

    part = value_terms(me, queries, jnp.concatenate(chunks, axis=0), grad_out)
    values = part[:rows]
    for k in range(1, shards):
        values = values + lax.ppermute(
            part[k * rows : (k + 1) * rows], "shard", [(s, s - k) for s in range(k, shards)]
        )
    values = values.astype(bf16)
    values_pair = swap(values, "shard", shards, 1)

    contract = (((0,), (0,)), ((), ()))
    product = lax.dot_general(
        jnp.concatenate([kept, arrived], axis=0),
        jnp.concatenate([values, values_pair], axis=0),
        contract,
        preferred_element_type=jnp.float32,
    )
    bits = [1 << n for n in range(replicas.bit_length() - 1)]
    split = tuple(2 for _ in bits)
    product = product.reshape((-1,) + split + (own_rows, columns))

    def scatter(x, order):
        left = sorted(order, reverse=True)
        for bit in order:
            mine, other = halve(x, 1 + left.index(bit), (rep // bit) % 2)
            x = mine + swap(other.astype(bf16), "rep", replicas, bit).astype(jnp.float32)
            left.remove(bit)
        return x

    mine, other = halve(product, len(bits), rep % 2)
    product = mine + swap(other.astype(bf16), "rep", replicas, 1).astype(jnp.float32)
    product = product.reshape((2, -1) + product.shape[1:])
    a = scatter(product[0], bits[1:])
    b = scatter(product[1], bits[:0:-1])
    gradient = jnp.concatenate([a, b], axis=0).reshape(
        shards // 2, new_capacity, own_rows, columns
    )
    pair = me // 2
    total = lax.dynamic_index_in_dim(gradient, pair, 0, keepdims=False)
    for k in range(1, shards // 2):
        out = lax.dynamic_index_in_dim(gradient, (pair + k) % (shards // 2), 0, keepdims=False)
        total = total + lax.ppermute(
            out.astype(bf16), "shard", [(s, (s + 2 * k) % shards) for s in range(shards)]
        ).astype(jnp.float32)
    gradient = total.transpose(1, 0, 2)

    param_new, first_new, second_new = adamw(param, first, second, gradient)
    working = param_new.astype(bf16)
    every = [working]
    for k in range(1, shards):
        every.append(
            lax.ppermute(working, "shard", [(s, (s + k) % shards) for s in range(shards)])
        )
    stacked = jnp.concatenate(every, axis=1)
    at = ((me - new_slot // new_capacity) % shards) * new_capacity + new_slot % new_capacity
    weights = spread(at[:, None] == jnp.arange(blocks)[None, :], stacked)
    return (param_new, first_new, second_new, weights)


def tables(old_ref, new_ref, tab_ref, old_capacity, capacity):
    count = old_ref.shape[1]
    sub = lax.broadcasted_iota(jnp.int32, (count, count), 0)
    lane = lax.broadcasted_iota(jnp.int32, (count, count), 1)

    def ranks(ref):
        across = jnp.broadcast_to(ref[...], (count, count))
        down = jnp.sum(jnp.where(sub == lane, across, 0), axis=1, keepdims=True)
        same = across == down
        below = jnp.sum(jnp.where(same & (lane < sub), 1, 0), axis=1, keepdims=True)
        return down, below

    old, old_rank = ranks(old_ref)
    new, new_rank = ranks(new_ref)
    hit = new * capacity + new_rank == lane
    old_rank = jnp.minimum(old_rank, old_capacity - 1)
    for at, table in enumerate((sub, old, old_rank)):
        tab_ref[at : at + 1, :count] = jnp.sum(jnp.where(hit, table, 0), axis=0, keepdims=True)


def fused_kernel(
    old_ref, new_ref, q_h, key_h, g_h, x_h, p_h, f_h, s_h,
    pn_h, fn_h, sn_h, wall_h,
    tab, tab_v, q_ref, g_ref, x_ref, state, kbuf, part, vo, v_in, vals, xs, xt, xo,
    st_own, st_first, raw_f0, raw_f1, raw_f2, first_out, first_in, raw_a1, raw_a2, raw_a3, raw_b0, raw_b1, raw_b2, raw_b3,
    r_out, a_in, l_out, l_in, d_out, d_in, settled,
    gbuf, pass_out, pass_in, mid_out, mid_in, fin_out, fin_in, grad, tmp, wall,
    load_sem, k_sem, x_sem, v_sem, va_sem, raw_sem, first_sem, st_sem,
    pass_sem, mid_sem, fin_sem, w_sem, sent,
):
    bf16, f32 = jnp.bfloat16, jnp.float32
    me, rep = lax.axis_index("shard"), lax.axis_index("rep")
    shards = kbuf.shape[1]
    rows = key_h.shape[0]
    length = shards * rows
    cap = pn_h.shape[1]
    blocks = xs.shape[1]
    own_rows = xs.shape[2]
    replicas = xs.shape[0]
    slots = cap * own_rows
    pieces = 4
    sources = shards - 1
    raw_a = (None, raw_a1, raw_a2, raw_a3)
    raw_f = (raw_f0, raw_f1, raw_f2)
    raw_b = (raw_b0, raw_b1, raw_b2, raw_b3)
    bits = (rep % 2, (rep // 2) % 2, rep // 4)
    has_left, has_right = me > 0, me < shards - 1
    edge = (me == 0) | (me == shards - 1)
    inner = (me > 0) & (me < shards - 1)
    pair = me + 1 - 2 * (me % 2)
    mid = shards - 1 - me
    side = me // 2
    near = 2 - side
    far = 3 - 3 * side
    left, right = (rep, me - 1), (rep, me + 1)

    def peer(k):
        return sum(
            (1 << n) * (bit + ((k >> n) & 1) * (1 - 2 * bit)) for n, bit in enumerate(bits)
        )

    def send(src, dst, sent, sem, target):
        return pltpu.make_async_remote_copy(
            src_ref=src, dst_ref=dst, send_sem=sent, recv_sem=sem,
            device_id=target, device_id_type=pl.DeviceIdType.MESH,
        )

    def wait_bytes(ref, sem):
        pltpu.make_async_copy(ref, ref, sem).wait()

    def cols(g):
        return pl.ds(g * HD, HD)

    def key_load(g):
        return pltpu.make_async_copy(key_h.at[:, cols(g)], kbuf.at[g, 0], load_sem.at[g])

    wide = x_h.shape[1] // pieces

    def x_load(p):
        span = pl.ds(p * wide, wide)
        return pltpu.make_async_copy(x_h.at[:, span], x_ref.at[:, span], load_sem.at[KV + p])

    late = KV + pieces
    q_load = pltpu.make_async_copy(q_h, q_ref, load_sem.at[late])
    g_load = pltpu.make_async_copy(g_h, g_ref, load_sem.at[late + 1])
    s_loads = [
        pltpu.make_async_copy(src, state.at[i], load_sem.at[late + 2 + i])
        for i, src in enumerate((p_h, f_h, s_h))
    ]
    for g in range(KV):
        key_load(g).start()
    for copy in s_loads:
        copy.start()
    for p in range(pieces):
        x_load(p).start()
    q_load.start()
    g_load.start()

    barrier = pltpu.get_barrier_semaphore()

    def greet(target):
        pl.semaphore_signal(barrier, inc=1, device_id=target, device_id_type=pl.DeviceIdType.MESH)

    for k in range(1, replicas):
        greet((peer(k), me))
    pl.when(has_left)(lambda: greet(left))
    pl.when(has_right)(lambda: greet(right))
    tables(old_ref, new_ref, tab_v, st_own.shape[1], cap)
    tab_load = pltpu.make_async_copy(tab_v, tab, load_sem.at[late + 5])
    tab_load.start()
    for g in range(KV):
        key_load(g).wait()
    tab_load.wait()
    pl.semaphore_wait(barrier, replicas + jnp.where(inner, 1, 0))

    def key_copy(g, j):
        return send(kbuf.at[g, j], kbuf.at[g, j + 1], sent.at[0], k_sem.at[g, j], right)

    for g in range(KV):
        pl.when(has_right)(lambda g=g: key_copy(g, 0).start())

    def key_relay(j):
        for g in range(KV):
            @pl.when((me >= j) & has_right)
            def _(g=g):
                key_copy(g, j - 1).wait_recv()
                if j < shards - 1:
                    key_copy(g, j).start()

            @pl.when(me < j)
            def _(g=g):
                kbuf[g, j] = jnp.zeros(kbuf.shape[2:], kbuf.dtype)

    for copy in s_loads:
        copy.wait()

    @pl.loop(0, st_own.shape[1])
    def _(s):
        for g in range(KV):
            for i in range(3):
                part_of = state[i, s, :, g * HD : (g + 1) * HD].astype(bf16)
                st_own[g, s, i] = part_of
                if g == 0:
                    st_first[i, s] = part_of

    def raw_right(g):
        return send(st_own.at[g], raw_a[g], sent.at[2], raw_sem.at[g, 0], right)

    def first_right(i):
        return send(st_first.at[i], raw_f[i], sent.at[4], first_sem.at[i, 0], right)

    def first_mid(i):
        return send(first_out.at[i], first_in.at[i], sent.at[5], first_sem.at[i, 1], right)

    def raw_left(g):
        return send(st_own.at[g], raw_b[g], sent.at[3], raw_sem.at[g, 1], left)

    def send_left(g):
        pl.when(me == sources - 1)(lambda: raw_left(g).start())

    for i in range(3):
        pl.when(me == 0)(lambda i=i: first_right(i).start())
    for g in range(1, KV):
        pl.when(me == 0)(lambda g=g: raw_right(g).start())
    for g in range(3):
        send_left(g)

    group = blocks // pieces

    def x_copy(p, k):
        span = pl.ds(p * group, group)
        return send(
            xs.at[peer(k), span],
            xt.at[span, :, pl.ds(pl.multiple_of(rep * rows, rows), rows)],
            sent.at[1],
            x_sem.at[0],
            (peer(k), me),
        )

    def x_keep(p):
        span = pl.ds(p * group, group)
        return pltpu.make_async_copy(
            xs.at[rep, span],
            xt.at[span, :, pl.ds(pl.multiple_of(rep * rows, rows), rows)],
            x_sem.at[1],
        )

    for p in range(pieces):
        x_load(p).wait()

        @pl.loop(p * group, (p + 1) * group, unroll=4)
        def _(b):
            block = x_ref[:, pl.ds(pl.multiple_of(b * HD, HD), HD)].T
            xs[:, b] = block.reshape(replicas, own_rows, rows)

        for k in (2, 4, 6, 3, 5, 7, 1):
            x_copy(p, k).start()
        x_keep(p).start()
        if p > 1:
            key_relay(p - 1)

    for j in range(pieces - 1, shards):
        key_relay(j)

    def v_copy(g, c):
        return send(vo.at[g, c], v_in.at[g, c], sent.at[6], v_sem.at[g, c], left)

    def va_copy(g, k):
        return send(vals.at[g, rep], vals.at[g, rep], sent.at[7], va_sem.at[g, k if k in (2, 4, 6) else 0], (peer(k), me))

    def va_relay(g, k):
        return send(vals.at[g, peer(k)], vals.at[g, peer(k)], sent.at[7], va_sem.at[g, 0], (peer(1), me))

    def finish(g, value):
        vals[g, rep] = value.astype(bf16)
        for k in (6, 2, 4, 1):
            va_copy(g, k).start()

    for i in range(3):
        @pl.when(me == 1)
        def _(i=i):
            first_right(i).wait_recv()
            for n, first in enumerate((3, 2)):
                @pl.loop(0, cap, unroll=4)
                def _(j):
                    s = first * cap + j
                    at = tab[2, s]
                    first_out[i, n, j] = jnp.where(tab[1, s] == 1, st_first[i, at], raw_f[i][at])

            first_mid(i).start()

    q_load.wait()
    g_load.wait()
    pack = 2
    token = lax.broadcasted_iota(jnp.int32, (length, pack * rows), 1) % rows
    place = lax.broadcasted_iota(jnp.int32, (length, pack * rows), 0)
    allowed = place <= jnp.where(place < rows, token, (me + 1) * rows - 1)

    @pl.loop(0, KV)
    def _(g):
        @pl.when(me == shards - 1)
        def _():
            for j in range(shards - 1):
                key_copy(g, j).wait_recv()

        keys = kbuf[g].reshape(length, HD)
        total = jnp.zeros((length, HD), f32)
        for h in range(0, GRP, pack):
            spans = [
                pl.ds(pl.multiple_of(g * (GRP * HD) + (h + i) * HD, HD), HD) for i in range(pack)
            ]
            queries = jnp.concatenate([q_ref[:, span] for span in spans], axis=0)
            scores = lax.dot_general(
                keys, queries, (((1,), (1,)), ((), ())), preferred_element_type=f32
            ) * HD ** (-0.5)
            scores = jnp.where(allowed, scores, -jnp.inf)
            weights = jnp.exp(scores - jnp.max(scores, axis=0, keepdims=True))
            share = 1.0 / jnp.sum(weights, axis=0, keepdims=True)
            total = total + jnp.dot(
                (weights * share).astype(bf16),
                jnp.concatenate([g_ref[:, span] for span in spans], axis=0),
                preferred_element_type=f32,
            )
        part[g] = total.reshape(shards, rows, HD)

        @pl.when(me == shards - 1)
        def _():
            for c in range(shards - 1):
                vo[g, c] = part[g, shards - 1 - c]
                v_copy(g, c).start()
            finish(g, part[g, 0])

    def chain(g, role):
        @pl.when(me == role)
        def _():
            for c in range(role):
                v_copy(g, c).wait_recv()
                vo[g, c] = part[g, role - c] + v_in[g, c]
                v_copy(g, c).start()
            v_copy(g, role).wait_recv()
            finish(g, part[g, 0] + v_in[g, role])

    def r_copy(g, i):
        return send(r_out.at[g, i], a_in.at[g, i], sent.at[8], st_sem.at[g, i], right)

    def l_copy(g):
        return send(l_out.at[g], l_in.at[g], sent.at[9], st_sem.at[g, 2], left)

    def d_copy(g):
        return send(d_out.at[g], d_in.at[g], sent.at[10], st_sem.at[g, 3], right)

    def choose(g, owner, first, out, other):
        @pl.loop(0, cap)
        def _(j):
            s = first * cap + j
            at = tab[2, s]
            out[j] = jnp.where(tab[1, s] == owner, st_own[g, at], other(j, at))

    def route_right(g):
        @pl.when(me == 1)
        def _():
            raw_right(g).wait_recv()
            for i, first in enumerate((3, 2)):
                choose(g, 1, first, r_out.at[g, i], lambda j, at: raw_a[g][at])
                r_copy(g, i).start()

    def route_left(g):
        @pl.when(me == 1)
        def _():
            raw_left(g).wait_recv()
            choose(g, 1, 0, l_out.at[g], lambda j, at: raw_b[g][at])
            l_copy(g).start()

    def route_last(g):
        @pl.when(me == 2)
        def _():
            if g > 0:
                r_copy(g, 0).wait_recv()
                choose(g, 2, 3, d_out.at[g], lambda j, at: a_in[g, 0, j])
            else:
                for i in range(3):
                    first_mid(i).wait_recv()

                @pl.loop(0, cap)
                def _(j):
                    s = 3 * cap + j
                    at = tab[2, s]
                    for i in range(3):
                        d_out[g, j, i] = jnp.where(tab[1, s] == 2, st_own[g, at, i], first_in[i, 0, j])

            d_copy(g).start()

    def settle(g):
        def take(other):
            @pl.loop(0, cap)
            def _(j):
                s = me * cap + j
                at = tab[2, s]
                mine = tab[1, s] == me
                moved = other(j, s, at)
                for i in range(3):
                    settled[i, j] = jnp.where(
                        mine, state[i, at, :, g * HD : (g + 1) * HD], moved[i].astype(f32)
                    )

        @pl.when(me == 0)
        def _():
            l_copy(g).wait_recv()
            take(lambda j, s, at: l_in[g, j])

        @pl.when(me == 1)
        def _():
            if g > 0:
                take(lambda j, s, at: jnp.where(tab[1, s] == 0, raw_a[g][at], raw_b[g][at]))
            else:
                take(
                    lambda j, s, at: [
                        jnp.where(tab[1, s] == 0, raw_f[i][at], raw_b[g][at, i]) for i in range(3)
                    ]
                )

        @pl.when(me == 2)
        def _():
            if g > 0:
                r_copy(g, 1).wait_recv()
                take(lambda j, s, at: a_in[g, 1, j])
            else:
                take(lambda j, s, at: [first_in[i, 1, j] for i in range(3)])

        @pl.when(me == 3)
        def _():
            d_copy(g).wait_recv()
            take(lambda j, s, at: d_in[g, j])

    def pass_copy(g, i):
        return send(pass_out.at[g, i], pass_in.at[g, i], sent.at[11], pass_sem.at[g, i], (rep, pair))

    def mid_copy(g, i):
        return send(mid_out.at[g, i], mid_in.at[g, i], sent.at[12], mid_sem.at[g, i], (rep, mid))

    def fin_copy(g):
        return send(fin_out.at[g], fin_in.at[g], sent.at[13], fin_sem.at[g], (rep, pair))

    def arrange():
        wait_bytes(xs.at[pl.ds(0, replicas - 1)], x_sem.at[0])
        wait_bytes(xs.at[0], x_sem.at[1])

        @pl.loop(0, blocks)
        def _(s):
            xo[s] = xt[tab[0, s]]

    def relay(g):
        for k in (2, 4, 6):
            va_copy(g, k).wait_recv()
            va_relay(g, k).start()

    def product(g):
        wait_bytes(vals.at[g, pl.ds(0, replicas // 2)], va_sem.at[g, 0])
        value = vals[g].reshape(replicas * rows, HD)

        @pl.loop(0, shards)
        def _(o):
            block = xo[pl.ds(o * cap, cap)].reshape(slots, replicas * rows)
            gbuf[g, o] = jnp.dot(block, value, preferred_element_type=f32)

        @pl.when(edge)
        def _():
            for i, to in enumerate((far, near)):
                pass_out[g, i] = gbuf[g, to].astype(bf16)
                pass_copy(g, i).start()

    def final(g, role):
        @pl.when(me == role)
        def _():
            fin_out[g] = gbuf[g, pair]
            fin_copy(g).start()

    def cross(g, role):
        @pl.when(me == role)
        def _():
            for i, to in enumerate((far, near)):
                pass_copy(g, i).wait_recv()
                mid_out[g, i] = (gbuf[g, to] + pass_in[g, i].astype(f32)).astype(bf16)
                mid_copy(g, i).start()

    def back(g, role):
        @pl.when(me == role)
        def _():
            mid_copy(g, 0).wait_recv()
            fin_out[g] = gbuf[g, pair] + mid_in[g, 0].astype(f32)
            fin_copy(g).start()

    def w_copy(g, t, direction):
        origin = (me - t, me + t)[direction]
        ref = wall.at[g, origin]
        return send(ref, ref, sent.at[14], w_sem.at[g, t, direction], (right, left)[direction])

    def w_out(g, origin):
        at = pl.ds(pl.multiple_of(origin * cap, cap), cap)
        return pltpu.make_async_copy(wall.at[g, origin], wall_h.at[:, at, cols(g)], sent.at[15])

    def update(g):
        settle(g)
        fin_copy(g).wait_recv()

        @pl.when(edge)
        def _():
            grad[...] = gbuf[g, me] + fin_in[g]

        @pl.when(inner)
        def _():
            mid_copy(g, 1).wait_recv()
            grad[...] = gbuf[g, me] + fin_in[g] + mid_in[g, 1].astype(f32)

        @pl.loop(0, cap)
        def _(j):
            at = pl.ds(pl.multiple_of(j * own_rows, own_rows), own_rows)
            new = adamw(settled[0, j], settled[1, j], settled[2, j], grad[at, :])
            for i in range(3):
                tmp[i, at, :] = new[i]

        for r in range(own_rows):
            param = tmp[0, pl.ds(r, cap, stride=own_rows), :]
            pn_h[r, :, g * HD : (g + 1) * HD] = param
            wall[g, me, r] = param.astype(bf16)
        pl.when(has_right)(lambda: w_copy(g, 0, 0).start())
        pl.when(has_left)(lambda: w_copy(g, 0, 1).start())
        for r in range(own_rows):
            for i in (1, 2):
                out = (fn_h, sn_h)[i - 1]
                out[r, :, g * HD : (g + 1) * HD] = tmp[i, pl.ds(r, cap, stride=own_rows), :]
        w_out(g, me).start()

    def gather_right(g, t):
        @pl.when(me >= t)
        def _():
            arrived = wall.at[g, me - t]
            send(arrived, arrived, sent.at[14], w_sem.at[g, t - 1, 0], right).wait_recv()
            if t < shards - 1:
                pl.when(has_right)(lambda: w_copy(g, t, 0).start())
            w_out(g, me - t).start()

    def gather_left(g, t):
        @pl.when(me + t < shards)
        def _():
            arrived = wall.at[g, me + t]
            send(arrived, arrived, sent.at[14], w_sem.at[g, t - 1, 1], left).wait_recv()
            if t < shards - 1:
                pl.when(has_left)(lambda: w_copy(g, t, 1).start())
            w_out(g, me + t).start()

    steps = [
        (route_last, 0), (route_left, 1), (chain, 0, 0), (chain, 0, 2), (route_right, 1), (route_right, 2),
        (chain, 0, 1), (send_left, 3), (route_left, 2), (chain, 1, 2), (arrange,), (relay, 0),
        (chain, 2, 2), (product, 0), (chain, 1, 1), (route_right, 3), (chain, 2, 1), (chain, 3, 2),
        (route_left, 3), (chain, 1, 0), (route_last, 1), (cross, 0, 2), (relay, 1), (chain, 2, 0),
        (route_last, 2), (final, 0, 0), (product, 1), (cross, 0, 1), (final, 1, 3), (relay, 2),
        (chain, 3, 1), (cross, 1, 2), (route_last, 3), (product, 2), (chain, 3, 0), (final, 2, 0),
        (cross, 2, 2), (route_left, 0), (relay, 3), (back, 0, 1), (back, 1, 1), (cross, 2, 1),
        (product, 3), (back, 0, 2), (cross, 3, 2), (back, 2, 2), (cross, 1, 1), (final, 0, 3),
        (final, 2, 3), (final, 1, 0), (back, 1, 2), (final, 3, 0), (update, 0), (back, 2, 1),
        (back, 3, 1), (cross, 3, 1), (back, 3, 2), (update, 2), (final, 3, 3), (update, 1),
        (gather_right, 0, 1), (gather_left, 0, 1), (update, 3), (gather_right, 0, 3), (gather_left, 1, 1), (gather_right, 3, 3),
        (gather_left, 2, 1), (gather_right, 2, 1), (gather_right, 0, 2), (gather_right, 3, 1), (gather_left, 0, 2), (gather_right, 1, 1),
        (gather_left, 3, 1), (gather_left, 2, 2), (gather_left, 0, 3), (gather_right, 1, 3), (gather_right, 1, 2), (gather_left, 3, 3),
        (gather_right, 3, 2), (gather_left, 1, 2), (gather_left, 1, 3), (gather_left, 3, 2), (gather_left, 2, 3), (gather_right, 2, 2),
        (gather_right, 2, 3),
    ]
    for step, *at in steps:
        step(*at)

    wait_bytes(xs.at[pl.ds(0, replicas - 1)], sent.at[1])
    wait_bytes(vals.at[:, pl.ds(0, replicas - 1)], sent.at[7])
    wait_bytes(fin_out, sent.at[13])
    wait_bytes(wall, sent.at[15])
    for role in range(shards):
        @pl.when(me == role)
        def _(role=role):
            if role < shards - 1:
                wait_bytes(kbuf.at[:, pl.ds(0, role + 1)], sent.at[0])
            if role > 0:
                wait_bytes(vo.at[:, pl.ds(0, role)], sent.at[6])
            if role in (0, shards - 1):
                wait_bytes(pass_out, sent.at[11])
                wait_bytes(wall.at[:, 0], sent.at[14])
            else:
                wait_bytes(mid_out, sent.at[12])
                moved = wall.shape[0] * (shards + 1) * wall.shape[2] * wall.shape[3] * wall.shape[4]
                wait_bytes(xs.at[pl.ds(0, moved // (blocks * own_rows * rows))], sent.at[14])
            if role == 0:
                wait_bytes(st_first, sent.at[4])
                wait_bytes(st_own.at[pl.ds(1, KV - 1)], sent.at[2])
            if role == 1:
                wait_bytes(first_out, sent.at[5])
                wait_bytes(r_out.at[pl.ds(1, KV - 1)], sent.at[8])
                wait_bytes(l_out, sent.at[9])
            if role == 2:
                wait_bytes(st_own, sent.at[3])
                wait_bytes(d_out, sent.at[10])


def finish_kernel(new_ref, pn_ref, fn_ref, sn_ref, wall_ref, pn_h, fn_h, sn_h, w_h, w_ref, sem):
    rows, blocks = w_ref.shape[:2]
    cap = pn_ref.shape[1]
    step = 4
    copies = [
        pltpu.make_async_copy(src, dst, sem.at[i])
        for i, (src, dst) in enumerate(((pn_ref, pn_h), (fn_ref, fn_h), (sn_ref, sn_h)))
    ]
    for copy in copies:
        copy.start()
    sub = lax.broadcasted_iota(jnp.int32, (blocks, blocks), 0)
    lane = lax.broadcasted_iota(jnp.int32, (blocks, blocks), 1)
    across = jnp.broadcast_to(new_ref[...], (blocks, blocks))
    owner = jnp.sum(jnp.where(sub == lane, across, 0), axis=1, keepdims=True)
    rank = jnp.sum(jnp.where((across == owner) & (lane < sub), 1, 0), axis=1, keepdims=True)
    hot = jnp.where(owner * cap + rank == lane, 1.0, 0.0).astype(w_ref.dtype)
    for n in range(rows // step):
        for r in range(n * step, (n + 1) * step):
            w_ref[r] = jnp.dot(hot, wall_ref[r], preferred_element_type=jnp.float32).astype(w_ref.dtype)
        span = pl.ds(n * step, step)
        copies.append(pltpu.make_async_copy(w_ref.at[span], w_h.at[span], sem.at[3 + n]))
        copies[-1].start()
    for copy in copies:
        copy.wait()


def fused(queries, keys, grad_out, inputs, old_owner, new_owner, param_old, first_old, second_old):
    shards = lax.axis_size("shard")
    replicas = lax.axis_size("rep")
    rows = queries.shape[0]
    blocks = old_owner.shape[0]
    own_rows = inputs.shape[1] // blocks // replicas
    cap = blocks // shards
    width = KV * HD
    old_cap = param_old.shape[1]
    bf16, f32 = jnp.bfloat16, jnp.float32
    pieces = 4

    V = pltpu.VMEM
    slot = V((own_rows, cap, width), f32)
    tokens = replicas * rows
    slots = cap * own_rows

    def state(*count):
        return V((*count, 3, own_rows, HD), bf16)

    def dma(*shape):
        return pltpu.SemaphoreType.DMA(shape)

    outs = pl.pallas_call(
        fused_kernel,
        out_shape=(slot, slot, slot, V((own_rows, blocks, width), bf16)),
        in_specs=[pl.BlockSpec(memory_space=pltpu.VMEM)] * 2 + [pl.BlockSpec(memory_space=pl.ANY)] * 7,
        out_specs=(pl.BlockSpec(memory_space=pltpu.VMEM),) * 4,
        scratch_shapes=[
            pltpu.SMEM((8, 128), jnp.int32), V((8, 128), jnp.int32),
            V(queries.shape, bf16), V(grad_out.shape, bf16), V(inputs.shape, bf16),
            V((3, old_cap, own_rows, width), f32),
            V((KV, shards, rows, HD), bf16),
            V((KV, shards, rows, HD), f32),
            V((KV, shards - 1, rows, HD), f32), V((KV, shards - 1, rows, HD), f32),
            V((KV, replicas, rows, HD), bf16),
            V((replicas, blocks, own_rows, rows), bf16),
            V((blocks, own_rows, tokens), bf16), V((blocks, own_rows, tokens), bf16),
            state(KV, old_cap), V((3, old_cap, own_rows, HD), bf16),
            *[V((old_cap, own_rows, HD), bf16)] * 3,
            *[V((3, 2, cap, own_rows, HD), bf16)] * 2,
            *[state(old_cap)] * 7,
            state(KV, 2, cap), state(KV, 2, cap),
            state(KV, cap), state(KV, cap), state(KV, cap), state(KV, cap),
            V((3, cap, own_rows, HD), f32),
            V((KV, shards, slots, HD), f32),
            *[V((KV, 2, slots, HD), bf16)] * 4,
            V((KV, slots, HD), f32), V((KV, slots, HD), f32),
            V((slots, HD), f32), V((3, slots, HD), f32),
            V((KV, shards, own_rows, cap, HD), bf16),
            dma(KV + pieces + 6), dma(KV, shards - 1), dma(2), dma(KV, shards - 1), dma(KV, replicas),
            dma(KV, 2), dma(3, 2), dma(KV, 4), dma(KV, 2), dma(KV, 2), dma(KV),
            dma(KV, shards - 1, 2), dma(16),
        ],
        compiler_params=pltpu.CompilerParams(
            collective_id=0, has_side_effects=True, vmem_limit_bytes=61 << 20
        ),
    )(
        old_owner[None], new_owner[None], queries, keys, grad_out, inputs,
        *[jnp.transpose(x, (1, 0, 2)) for x in (param_old, first_old, second_old)],
    )
    return pl.pallas_call(
        finish_kernel,
        out_shape=tuple(
            jax.ShapeDtypeStruct((own_rows, count, width), kind)
            for count, kind in ((cap, f32), (cap, f32), (cap, f32), (blocks, bf16))
        ),
        in_specs=[pl.BlockSpec(memory_space=pltpu.VMEM)] * 5,
        out_specs=(pl.BlockSpec(memory_space=pl.ANY),) * 4,
        scratch_shapes=[V((own_rows, blocks, width), bf16), dma(own_rows // 4 + 3)],
        compiler_params=pltpu.CompilerParams(vmem_limit_bytes=8 << 20),
    )(new_owner[None], *[pltpu.with_memory_space_constraint(x, pltpu.VMEM) for x in outs])


def solution(mesh):
    placed = (
        P(("rep", "shard"), None),
        P(("rep", "shard"), None),
        P(("rep", "shard"), None),
        P(("rep", "shard"), None),
        P(),
        P(),
        P("rep", "shard", None),
        P("rep", "shard", None),
        P("rep", "shard", None),
    )
    small = mesh.shape["shard"] == 4 and mesh.shape["rep"] == 8
    return jax.shard_map(
        fused if small else local,
        mesh=mesh,
        in_specs=placed,
        out_specs=(
            P("rep", "shard", None),
            P("rep", "shard", None),
            P("rep", "shard", None),
            P("rep", None, None),
        ),
        check_vma=False,
    )
```
